128 devices in a mesh: src: 16 (over y, x), tgt: 8 (over z, core).
Axes of the slice: x: 4, y: 4, z: 4, core: 2. Of those that a mesh axis runs over, the one named last changes fastest.
Arguments:
- src_points: bfloat16 [32768, 1024], P(('src', 'tgt')), may hold values from -6 to 6
- tgt_points: bfloat16 [32768, 1024], P(('src', 'tgt')), may hold values from -24 to 24
- src_factor: bfloat16 [32768, 256], P(('src', 'tgt')), may hold values from 0.25 to 4
- tgt_factor: bfloat16 [32768, 256], P(('src', 'tgt')), may hold values from 0.25 to 4
- inner_marginal: float32 [256], replicated, may hold values from 0.3 to 3
- src_cluster: int32 [32768], P(('src', 'tgt')), may hold values from 0 to 255, as said below
- tgt_cluster: int32 [32768], P(('src', 'tgt')), may hold values from 0 to 255, as said below
Outputs:
- src_update: bfloat16 [32768, 256], P(('src', 'tgt'))
- tgt_update: bfloat16 [32768, 256], P(('src', 'tgt'))
- mapped: bfloat16 [32768, 1024], P(('src', 'tgt'))
The draws below stay inside these ranges and needn't reach their ends.
Inputs may be any that keep to these rules, and one draw needn't show every extreme that they name: `src_cluster`: Co-cluster c belongs to the owner c // 2 (devices in the order of src+tgt). Over the 256 source points of one device, the points whose co-cluster belongs to one owner number at most 4, and at least one for every owner; some owner receives exactly 4 from every device. `tgt_cluster`: Co-cluster c belongs to the owner c // 2. Over the 256 target points of one device, the points whose co-cluster belongs to one owner number at most 4, and at least one for every owner; some owner receives exactly 4 from every device. Every co-cluster holds at least one target point.
All inputs are finite; a program needn't handle non-finite values. Where the reference program divides by a largest or mean magnitude, that divisor is 1e-20 or more.
Results may differ from the reference program's by a relative error of at most 0.0049.
Values may be sent and summed in bfloat16 or wider, within the bound.
A program may use at most 64 MiB of HBM per device.

```python
import math
import jax
import jax.numpy as jnp
from jax import lax

D = 1024
R = 256
ROWS = 256
CL_DEV = 2
CAP = 4
POINTS = 32768
DEVICES = 128


def cluster_draw(key, salt):
    salted = jax.random.fold_in(key, salt)
    heavy = jax.random.randint(jax.random.fold_in(salted, 1), (), 0, DEVICES)
    slot_count = DEVICES * CAP
    slot_ids = jnp.arange(slot_count, dtype=jnp.int32)
    forced = jnp.logical_or(slot_ids // CAP == heavy, slot_ids % CAP == 0)

    def one_block(block_id):
        block_key = jax.random.fold_in(salted, 100 + block_id)
        ordering = jax.random.permutation(jax.random.fold_in(block_key, 1), slot_count).astype(jnp.int32)
        priority = jnp.where(forced, slot_count, 0) + ordering
        chosen = jnp.argsort(-priority)[:ROWS].astype(jnp.int32)
        mixing = jax.random.permutation(jax.random.fold_in(block_key, 2), ROWS)
        chosen = chosen[mixing]
        owners = chosen // CAP
        picks = jax.random.randint(jax.random.fold_in(block_key, 3), (ROWS,), 0, CL_DEV)
        picks = jnp.where(chosen % CAP == 0, block_id % CL_DEV, picks)
        return owners * CL_DEV + picks
    blocks = lax.map(one_block, jnp.arange(DEVICES, dtype=jnp.int32))
    return blocks.reshape(-1).astype(jnp.int32)


def draw_src_cluster(key, part):
    return cluster_draw(key, 5)


def draw_tgt_cluster(key, part):
    return cluster_draw(key, 6)


def block_scale(stream_key, dims, cuts, low, top_value):
    def one(position, blocks):
        draws = jax.random.uniform(jax.random.fold_in(jax.random.fold_in(stream_key, 6), position), (blocks,), jnp.float32, low / len(cuts), top_value / len(cuts))
        return jnp.repeat(jnp.exp(draws), dims[position] // blocks).reshape((-1,) + (1,) * (len(dims) - position - 1))

    gain = one(*cuts[0])
    for cut in cuts[1:]:
        gain = gain * one(*cut)
    return gain


def bell_draw(key, dims, spread, limit, cuts=(), held_as=jnp.bfloat16):
    values = jax.random.normal(key, dims, jnp.float32) * spread
    if len(cuts) > 0:
        values = block_scale(key, dims, cuts, -0.22, 0.18) * values
    return jnp.clip(values, min=-limit, max=limit).astype(held_as)


def setup_inputs(seed: int = 0) -> dict:
    streams_of = jax.random.split(jax.random.key(seed), 8)
    src_points = bell_draw(streams_of[0], (POINTS, D), 1.0, 6.0, ((0, 128),))
    tgt_points = bell_draw(streams_of[1], (POINTS, D), 4.0, 24.0, ((0, 128),))
    src_factor = jnp.clip(jnp.exp(math.log(4.0) - 2.7725887 * jax.random.uniform(streams_of[2], (POINTS, R), jnp.float32) ** block_scale(streams_of[2], (POINTS, R), ((0, 128),), -0.2, 0.2)), 0.25, 4.0).astype(jnp.bfloat16)
    tgt_factor = jnp.clip(jnp.exp(math.log(4.0) - 2.7725887 * jax.random.uniform(streams_of[3], (POINTS, R), jnp.float32) ** block_scale(streams_of[3], (POINTS, R), ((0, 128),), -0.2, 0.2)), 0.25, 4.0).astype(jnp.bfloat16)
    inner_marginal = jnp.clip(jnp.exp(jax.random.uniform(streams_of[4], (R,), jnp.float32, math.log(0.3), math.log(3.0))), 0.3, 3.0)
    src_cluster = draw_src_cluster(jax.random.fold_in(streams_of[7], 71), 0)
    tgt_cluster = draw_tgt_cluster(jax.random.fold_in(streams_of[7], 71), 0)
    return {"src_points": src_points, "tgt_points": tgt_points, "src_factor": src_factor, "tgt_factor": tgt_factor, "inner_marginal": inner_marginal, "src_cluster": src_cluster, "tgt_cluster": tgt_cluster}


GAMMA = 2.0
TEMPER = 0.03
EPS = 1e-06

def mirror_step(points, total, factor, inner_marginal):
    total_round = total.astype(jnp.bfloat16)
    gradient = -jnp.dot(points, total_round, preferred_element_type=jnp.float32) / inner_marginal[None, :]
    row_scale = lax.optimization_barrier(jnp.max(jnp.abs(gradient), axis=1, keepdims=True)) + EPS
    tilted = factor.astype(jnp.float32) * jnp.exp(-GAMMA * gradient / row_scale)
    return (tilted / lax.optimization_barrier(jnp.mean(tilted, axis=1, keepdims=True))).astype(jnp.bfloat16)

def layout(owners):
    ordering = jnp.argsort(owners, stable=True).astype(jnp.int32)
    counts = jax.ops.segment_sum(jnp.ones_like(owners), owners, num_segments=DEVICES).astype(jnp.int32)
    starts = (jnp.cumsum(counts) - counts).astype(jnp.int32)
    padded = jnp.concatenate([ordering, jnp.full((2 * ROWS,), POINTS, jnp.int32)])
    return (padded, starts, counts)

def reference(src_points, tgt_points, src_factor, tgt_factor, inner_marginal, src_cluster, tgt_cluster):
    tgt_sum = jnp.dot(tgt_points.T, tgt_factor, preferred_element_type=jnp.float32)
    src_sum = jnp.dot(src_points.T, src_factor, preferred_element_type=jnp.float32)
    src_update = mirror_step(src_points, tgt_sum, src_factor, inner_marginal)
    tgt_update = mirror_step(tgt_points, src_sum, tgt_factor, inner_marginal)
    src_pad, src_start, src_count = layout((src_cluster // CL_DEV).astype(jnp.int32))
    tgt_pad, tgt_start, tgt_count = layout((tgt_cluster // CL_DEV).astype(jnp.int32))
    buffer_len = 2 * ROWS
    inv_src = lax.rsqrt(lax.optimization_barrier(jnp.sum(jnp.square(src_points.astype(jnp.float32)), axis=1)) + EPS)
    inv_tgt = lax.rsqrt(lax.optimization_barrier(jnp.sum(jnp.square(tgt_points.astype(jnp.float32)), axis=1)) + EPS)
    positions = jnp.arange(buffer_len, dtype=jnp.int32)

    def one_owner(result, owner_id):
        src_idx = lax.dynamic_slice(src_pad, (src_start[owner_id].astype(jnp.int32),), (buffer_len,))
        src_ok = positions < src_count[owner_id]
        src_safe = jnp.where(src_ok, src_idx, 0)
        tgt_idx = lax.dynamic_slice(tgt_pad, (tgt_start[owner_id].astype(jnp.int32),), (buffer_len,))
        tgt_ok = positions < tgt_count[owner_id]
        tgt_safe = jnp.where(tgt_ok, tgt_idx, 0)
        src_rows = src_points[src_safe]
        tgt_rows = tgt_points[tgt_safe]
        src_labels = jnp.where(src_ok, src_cluster[src_safe], -2)
        tgt_labels = jnp.where(tgt_ok, tgt_cluster[tgt_safe], -1)
        products = jnp.dot(src_rows, tgt_rows.T, preferred_element_type=jnp.float32)
        cosine = products * inv_src[src_safe][:, None] * inv_tgt[tgt_safe][None, :]
        weight = jnp.dot(src_update[src_safe], tgt_update[tgt_safe].T, preferred_element_type=jnp.float32) / R
        kernel = jnp.where(src_labels[:, None] == tgt_labels[None, :], weight * jnp.exp((cosine - 1.0) / TEMPER), 0.0)
        denominator = lax.optimization_barrier(jnp.sum(kernel, axis=1, keepdims=True))
        denominator = jnp.where(denominator > 0, denominator, 1.0)
        transport = (kernel / denominator).astype(jnp.bfloat16)
        images = jnp.dot(transport, tgt_rows, preferred_element_type=jnp.float32).astype(jnp.bfloat16)
        result = result.at[jnp.where(src_ok, src_idx, POINTS)].set(images, mode='drop')
        return (result, None)
    mapped, _ = lax.scan(one_owner, jnp.zeros((POINTS, D), jnp.bfloat16), jnp.arange(DEVICES, dtype=jnp.int32))
    return (src_update, tgt_update, mapped)
```

```python
import jax
import jax.numpy as jnp
from jax import lax
from jax.experimental import pallas as pl
from jax.experimental.pallas import tpu as pltpu
from jax.sharding import PartitionSpec as P

CL_DEV = 2
CAP = 4
GAMMA = 2.0
TEMPER = 0.03
EPS = 1e-06

D = 1024
R = 256
ROWS = 256
NDEV = 128
SLOTS = NDEV * CAP
QUART = D // 4
GROUP = 16
NGROUP = NDEV // GROUP
MESH = pl.DeviceIdType.MESH
BF = jnp.bfloat16
F32 = jnp.float32
I32 = jnp.int32


def offset_of(k):
    x1, y1, z1, x0, y0, z0, c = ((k >> b) & 1 for b in (6, 5, 4, 3, 2, 1, 0))
    return (y1 * 8 + y0 * 4 + x1 * 2 + x0, z1 * 4 + z0 * 2 + c)


def hops(k):
    ds, dt = offset_of(k)
    ring = (0, 1, 2, 1)
    return ring[ds // 4] + ring[ds % 4] + ring[dt // 2]


def place_of(owner):
    bit = lambda b: (owner // (1 << b)) % 2
    y1, y0, x1, x0, z1, z0, c = (bit(b) for b in (6, 5, 4, 3, 2, 1, 0))
    return x1 * 64 + y1 * 32 + z1 * 16 + x0 * 8 + y0 * 4 + z0 * 2 + c


def flips(value, bits):
    parts = [(value // (1 << b)) % 2 for b in range(bits)]
    out = []
    for m in range(1 << bits):
        total = 0
        for b in range(bits):
            total = total + ((1 - parts[b]) if (m >> b) & 1 else parts[b]) * (1 << b)
        out.append(total)
    return out


def dot(a, b, dims=((1,), (0,)), precision=None):
    return lax.dot_general(a, b, (dims, ((), ())), preferred_element_type=F32, precision=precision)


def iota(shape, axis):
    return lax.broadcasted_iota(I32, shape, axis)


def mirror(points, total_t, factor, marginal):
    gradient = dot(points, total_t, ((1,), (1,))) / marginal
    row_scale = jnp.max(jnp.abs(gradient), axis=1, keepdims=True) + EPS
    tilted = factor.astype(F32) * jnp.exp(GAMMA * gradient / row_scale)
    mean = jnp.mean(tilted, axis=1, keepdims=True)
    return (tilted / jnp.where(mean > 0, mean, 1.0)).astype(BF)


def slots_of(cluster_row, me_bits):
    eye = iota((ROWS, ROWS), 0) == iota((ROWS, ROWS), 1)
    owner_row = cluster_row // CL_DEV
    cluster_col = jnp.sum(jnp.where(eye, cluster_row, 0).astype(F32), axis=1, keepdims=True).astype(I32)
    owner_col = cluster_col // CL_DEV
    same = owner_col == owner_row
    below = iota((ROWS, ROWS), 0) < iota((ROWS, ROWS), 1)
    above = iota((ROWS, ROWS), 1) < iota((ROWS, ROWS), 0)
    rank_row = jnp.sum(jnp.where(same & below, 1.0, 0.0), axis=0, keepdims=True).astype(I32)
    rank_col = jnp.sum(jnp.where(same & above, 1.0, 0.0), axis=1, keepdims=True).astype(I32)

    def block(owner):
        place = place_of(owner)
        total = 0
        for b in range(7):
            mine = me_bits[b]
            theirs = (place // (1 << b)) % 2
            total = total + (mine + theirs - 2 * mine * theirs) * (1 << b)
        return total

    return block(owner_row), rank_row, block(owner_col), rank_col, cluster_col


def kernel(
    sp, tp, sf, tf, marg, scl, tcl,
    su, tu, mp,
    pf, pp, rx, cs, rr, mm, ts, tr, ss, sr, ls, lr, tall, ball, sfall, irow, lcol, lrow, isend, irecv,
    pair_s, pair_r, rs_s, rs_r, ag_s, ag_r, pb_s, pb_r, lab_s, lab_r, tg_s, tg_r, sc_s, sc_r, rt_s, rt_r,
):
    s = lax.axis_index("src")
    t = lax.axis_index("tgt")
    z = t // 2
    core = t % 2
    sx = flips(s, 4)
    tx = flips(t, 3)
    zx = flips(z, 2)

    def peer(k):
        ds, dt = offset_of(k)
        return (sx[ds], tx[dt])

    partner = (s, tx[1])

    barrier = pltpu.get_barrier_semaphore()
    for k in range(1, NDEV):
        pl.semaphore_signal(barrier, inc=1, device_id=peer(k), device_id_type=MESH)

    part = dot(tf[...], tp[...], ((0,), (0,)))
    pf[0] = part
    pp[0] = part.astype(BF)
    part = dot(sf[...], sp[...], ((0,), (0,)))
    pf[1] = part
    pp[1] = part.astype(BF)

    me = s * 8 + t
    mp_place = place_of(me)
    me_bits = [(mp_place // (1 << b)) % 2 for b in range(7)]
    s_blk_row, s_rank_row, s_blk_col, s_rank_col, s_cl_col = slots_of(scl[...], me_bits)
    t_blk_row, t_rank_row, t_blk_col, t_rank_col, t_cl_col = slots_of(tcl[...], me_bits)
    s_slot_row = s_blk_row * CAP + s_rank_row
    t_slot_row = t_blk_row * CAP + t_rank_row
    s_slot_col = s_blk_col * CAP + s_rank_col

    lane = iota((ROWS, NDEV), 1)
    blk = iota((NDEV, ROWS), 0)
    s_val = jnp.where(lane == s_rank_col, (s_cl_col % CL_DEV + 1).astype(F32), 0.0).astype(BF)
    t_val = jnp.where(lane == t_rank_col + CAP, (t_cl_col % CL_DEV + 1).astype(F32), 0.0).astype(BF)
    s_hot = jnp.where(blk == s_blk_row, 1.0, 0.0).astype(BF)
    t_hot = jnp.where(blk == t_blk_row, 1.0, 0.0).astype(BF)
    labels = (dot(s_hot, s_val) + dot(t_hot, t_val)).astype(I32)
    ls[...] = labels.reshape(NDEV, 1, NDEV)

    row = iota((ROWS, ROWS), 0)
    col = iota((ROWS, ROWS), 1)
    to_wire = jnp.where(col == (row // 4 % 4) * 64 + (row // 16) * 4 + row % 4, 1.0, 0.0).astype(BF)
    from_wire = jnp.where(row == (col // 4 % 4) * 64 + (col // 16) * 4 + col % 4, 1.0, 0.0).astype(BF)

    def hot_rows(b, slot_row):
        return jnp.where(iota((64, ROWS), 0) + b * 64 == slot_row, 1.0, 0.0).astype(BF)

    def quarters(x):
        return jnp.concatenate([x[:, q * QUART : (q + 1) * QUART] for q in range(4)], axis=0)

    def pack_tgt(b, carry):
        t_sel = hot_rows(b, t_slot_row)
        s_sel = hot_rows(b, s_slot_row)
        rows = dot(t_sel, tp[...]).astype(BF)
        f_t = dot(t_sel, tf[...]).astype(BF)
        f_s = dot(s_sel, sf[...]).astype(BF)
        facs = jnp.concatenate([f_s[:, :128], f_s[:, 128:], f_t[:, :128], f_t[:, 128:]], axis=0)
        at = pl.ds(pl.multiple_of(b * 256, 256), 256)
        ts[at, 0:QUART] = dot(to_wire, quarters(rows)).astype(BF)
        ts[at, QUART : QUART + 128] = dot(to_wire, facs).astype(BF)
        return carry

    def pack_src(b, carry):
        rows = dot(hot_rows(b, s_slot_row), sp[...]).astype(BF)
        at = pl.ds(pl.multiple_of(b * 256, 256), 256)
        ss[at, :] = dot(to_wire, quarters(rows)).astype(BF)
        return carry

    lax.fori_loop(0, NGROUP, pack_tgt, 0)

    pl.semaphore_wait(barrier, NDEV - 1)

    def remote(src, dst, send, recv, device):
        return pltpu.make_async_remote_copy(
            src_ref=src, dst_ref=dst, send_sem=send, recv_sem=recv, device_id=device, device_id_type=MESH
        )

    pair = remote(pp.at[1 - core], rx, pair_s, pair_r, partner)
    pair.start()

    lax.fori_loop(0, NGROUP, pack_src, 0)
    tr[0:16, :] = ts[0:16, :]
    sr[0:16, :] = ss[0:16, :]
    lr[0] = ls[0]

    pair.wait_recv()
    cs[...] = (pf[core] + rx[...].astype(F32)).astype(BF)

    for kc in range(1, 64):
        ds, dz = kc // 4, kc % 4
        remote(
            cs.at[pl.ds(pl.multiple_of(sx[ds] * 16, 16), 16), pl.ds(pl.multiple_of(zx[dz] * 256, 256), 256)],
            rr.at[kc], rs_s, rs_r, (sx[ds], tx[dz * 2]),
        ).start()

    order = sorted(range(1, NDEV), key=lambda k: (-(k // GROUP), -hops(k)))
    for k in order:
        at = pl.ds(k * 16, 16)
        remote(ts.at[at], tr.at[at], tg_s, tg_r, peer(k)).start()
        remote(ls.at[k], lr.at[k], lab_s, lab_r, peer(k)).start()

    rest = rr.at[pl.ds(1, 63)]
    remote(rest, rest, rs_s, rs_r, partner).wait_recv()
    my_rows = pl.ds(pl.multiple_of(s * 16, 16), 16)
    my_cols = pl.ds(pl.multiple_of(z * 256, 256), 256)
    total = cs[my_rows, my_cols].astype(F32)
    for kc in range(1, 64):
        total = total + rr[kc].astype(F32)
    mm[core, my_rows, my_cols] = total.astype(BF)

    mine = mm.at[core, my_rows, my_cols]
    for kc in range(1, 64):
        ds, dz = kc // 4, kc % 4
        remote(mine, mine, ag_s, ag_r, (sx[ds], tx[dz * 2])).start()
    for k in order:
        at = pl.ds(k * 16, 16)
        g = k // GROUP
        remote(ss.at[at], sr.at[at], sc_s.at[g], sc_r.at[g], peer(k)).start()
    remote(rest, rest, ag_s, ag_r, partner).wait_recv()
    pair_back = remote(mm.at[core], mm.at[core], pb_s, pb_r, partner)
    pair_back.start()
    remote(mm.at[1 - core], mm.at[1 - core], pb_s, pb_r, partner).wait_recv()

    marginal = marg[...]
    su[...] = mirror(sp[...], mm[0], sf[...], marginal)
    tu[...] = mirror(tp[...], mm[1], tf[...], marginal)

    tgt_rest = pl.ds(16, 2032)
    remote(ts.at[tgt_rest], tr.at[tgt_rest], tg_s, tg_r, partner).wait_recv()
    lab_rest = pl.ds(1, 127)
    remote(ls.at[lab_rest], lr.at[lab_rest], lab_s, lab_r, partner).wait_recv()

    def owner_tgt(b, carry):
        at = pl.ds(pl.multiple_of(b * 256, 256), 256)
        to = pl.ds(pl.multiple_of(b * 64, 64), 64)
        rows = dot(from_wire, tr[at, 0:QUART]).astype(BF)
        facs = dot(from_wire, tr[at, QUART : QUART + 128]).astype(BF)
        points = jnp.concatenate([rows[q * 64 : (q + 1) * 64] for q in range(4)], axis=1)
        tall[to, :] = points
        sfall[to, :] = jnp.concatenate([facs[0:64], facs[64:128]], axis=1)
        tgt_fac = jnp.concatenate([facs[128:192], facs[192:256]], axis=1)
        ball[to, :] = mirror(points, mm[1], tgt_fac, marginal)
        return carry

    lax.fori_loop(0, NGROUP, owner_tgt, 0)

    squares = jnp.zeros((SLOTS, 128), F32)
    for j in range(D // 128):
        piece = tall[:, j * 128 : (j + 1) * 128].astype(F32)
        squares = squares + piece * piece
    ones = jnp.ones((8, 128), F32)
    sums = dot(ones, squares, ((1,), (1,)), precision=lax.Precision.HIGHEST)
    irow[...] = lax.rsqrt(sums + EPS)

    got = lr[...].reshape(NDEV, NDEV).astype(F32).astype(BF)
    spread = jnp.where(iota((SLOTS, NDEV), 0) // CAP == iota((SLOTS, NDEV), 1), 1.0, 0.0).astype(BF)
    per_slot = dot(spread, got)
    slot_lane = iota((SLOTS, NDEV), 1) - iota((SLOTS, NDEV), 0) % CAP
    lcol[...] = jnp.broadcast_to(
        jnp.sum(jnp.where(slot_lane == 0, per_slot, 0.0), axis=1, keepdims=True), (SLOTS, NDEV)
    )
    tgt_lab = jnp.where(slot_lane == CAP, per_slot, 0.0).astype(BF)
    lrow[...] = dot(jnp.ones((8, NDEV), BF), tgt_lab, ((1,), (1,)))

    STEP = 2
    span = 64 * STEP

    def owner_src(first):
        at0 = first * 64
        pieces = []
        for j in range(STEP):
            at = slice((first + j) * 256, (first + j + 1) * 256)
            rows = dot(from_wire, sr[at, :]).astype(BF)
            pieces.append(jnp.concatenate([rows[q * 64 : (q + 1) * 64] for q in range(4)], axis=1))
        points = jnp.concatenate(pieces, axis=0)
        update = mirror(points, mm[0], sfall[at0 : at0 + span, :], marginal)
        squares = jnp.zeros((span, 128), F32)
        for j in range(D // 128):
            piece = points[:, j * 128 : (j + 1) * 128].astype(F32)
            squares = squares + piece * piece
        inv_src = lax.rsqrt(jnp.sum(squares, axis=1, keepdims=True) + EPS)
        cosine = dot(points, tall[...], ((1,), (1,))) * inv_src * irow[0:1, :]
        weight = dot(update, ball[...], ((1,), (1,))) / R
        same = lcol[at0 : at0 + span, 0:1] == lrow[0:1, :]
        kern = jnp.where(same, weight * jnp.exp((cosine - 1.0) / TEMPER), 0.0)
        denominator = jnp.sum(kern, axis=1, keepdims=True)
        denominator = jnp.where(denominator > 0, denominator, 1.0)
        transport = (kern / denominator).astype(BF)
        image = dot(transport, tall[...]).astype(BF)
        for j in range(STEP):
            at = slice((first + j) * 256, (first + j + 1) * 256)
            isend[at, :] = dot(to_wire, quarters(image[j * 64 : (j + 1) * 64])).astype(BF)

    def group_rows(g):
        return pl.ds(16, 240) if g == 0 else pl.ds(g * 256, 256)

    for first in range(NGROUP - STEP, -1, -STEP):
        for g in range(first, first + STEP):
            remote(ss.at[group_rows(g)], sr.at[group_rows(g)], sc_s.at[g], sc_r.at[g], partner).wait_recv()
        owner_src(first)
        if first == 0:
            irecv[0:16, :] = isend[0:16, :]
        for k in order:
            g = k // GROUP
            if first <= g < first + STEP:
                at = pl.ds(k * 16, 16)
                remote(isend.at[at], irecv.at[at], rt_s.at[g], rt_r.at[g], peer(k)).start()

    mapped = jnp.zeros((ROWS, D), F32)
    for first in range(NGROUP - 4, -1, -4):
        blocks = []
        for g in range(first, first + 4):
            remote(isend.at[group_rows(g)], irecv.at[group_rows(g)], rt_s.at[g], rt_r.at[g], partner).wait_recv()
            rows = dot(from_wire, irecv[g * 256 : (g + 1) * 256, :]).astype(BF)
            blocks.append(jnp.concatenate([rows[q * 64 : (q + 1) * 64] for q in range(4)], axis=1))
        images = jnp.concatenate(blocks, axis=0)
        pick = jnp.where(iota((ROWS, 256), 1) + first * 64 == s_slot_col, 1.0, 0.0).astype(BF)
        mapped = mapped + dot(pick, images)
    mp[...] = mapped.astype(BF)

    pair.wait_send()
    remote(rest, rest, rs_s, rs_r, partner).wait_send()
    remote(rest, rest, ag_s, ag_r, partner).wait_send()
    pair_back.wait_send()
    remote(ts.at[tgt_rest], tr.at[tgt_rest], tg_s, tg_r, partner).wait_send()
    remote(ls.at[lab_rest], lr.at[lab_rest], lab_s, lab_r, partner).wait_send()
    for g in range(NGROUP):
        remote(ss.at[group_rows(g)], sr.at[group_rows(g)], sc_s.at[g], sc_r.at[g], partner).wait_send()
        remote(isend.at[group_rows(g)], irecv.at[group_rows(g)], rt_s.at[g], rt_r.at[g], partner).wait_send()


def per_device(src_points, tgt_points, src_factor, tgt_factor, inner_marginal, src_cluster, tgt_cluster):
    dma = pltpu.SemaphoreType.DMA
    vmem = pl.BlockSpec(memory_space=pltpu.VMEM)
    return pl.pallas_call(
        kernel,
        out_shape=(
            jax.ShapeDtypeStruct((ROWS, R), BF),
            jax.ShapeDtypeStruct((ROWS, R), BF),
            jax.ShapeDtypeStruct((ROWS, D), BF),
        ),
        in_specs=[vmem] * 7,
        out_specs=(vmem,) * 3,
        scratch_shapes=[
            pltpu.VMEM((2, R, D), F32),
            pltpu.VMEM((2, R, D), BF),
            pltpu.VMEM((R, D), BF),
            pltpu.VMEM((R, D), BF),
            pltpu.VMEM((64, 16, 256), BF),
            pltpu.VMEM((2, R, D), BF),
            pltpu.VMEM((NDEV * 16, 384), BF),
            pltpu.VMEM((NDEV * 16, 384), BF),
            pltpu.VMEM((NDEV * 16, 256), BF),
            pltpu.VMEM((NDEV * 16, 256), BF),
            pltpu.VMEM((NDEV, 1, NDEV), I32),
            pltpu.VMEM((NDEV, 1, NDEV), I32),
            pltpu.VMEM((SLOTS, D), BF),
            pltpu.VMEM((SLOTS, R), BF),
            pltpu.VMEM((SLOTS, R), BF),
            pltpu.VMEM((8, SLOTS), F32),
            pltpu.VMEM((SLOTS, NDEV), F32),
            pltpu.VMEM((8, SLOTS), F32),
            pltpu.VMEM((NDEV * 16, 256), BF),
            pltpu.VMEM((NDEV * 16, 256), BF),
        ]
        + [dma] * 12
        + [dma((NGROUP,))] * 4,
        compiler_params=pltpu.CompilerParams(collective_id=0, has_side_effects=True, vmem_limit_bytes=60 << 20),
        name="transport",
    )(
        src_points,
        tgt_points,
        src_factor,
        tgt_factor,
        inner_marginal.reshape(1, R),
        src_cluster.reshape(1, ROWS),
        tgt_cluster.reshape(1, ROWS),
    )


def solution(mesh):
    both = P(("src", "tgt"), None)
    flat = P(("src", "tgt"))
    return jax.shard_map(
        per_device,
        mesh=mesh,
        in_specs=(both, both, both, both, P(), flat, flat),
        out_specs=(both, both, both),
        check_vma=False,
    )
```

```python
import jax
import jax.numpy as jnp
from jax import lax
from jax.experimental import pallas as pl
from jax.experimental.pallas import tpu as pltpu
from jax.sharding import PartitionSpec as P

CL_DEV = 2
CAP = 4
GAMMA = 2.0
TEMPER = 0.03
EPS = 1e-06

D = 1024
R = 256
ROWS = 256
NDEV = 128
SLOTS = NDEV * CAP
QUART = D // 4
GROUP = 16
NGROUP = NDEV // GROUP
GROUPS = tuple(range(NGROUP - 1, -1, -1))
PACK_EARLY = 2
SENT_FIRST = 2
PACK_PAIR = 4
SENT_SECOND = 5
STEP = 2
LAST = 2
VLIM = 56 << 20
MESH = pl.DeviceIdType.MESH
BF = jnp.bfloat16
F32 = jnp.float32
I32 = jnp.int32


def offset_of(k):
    x1, y1, z1, x0, y0, z0, c = ((k >> b) & 1 for b in (6, 5, 4, 3, 2, 1, 0))
    return (y1 * 8 + y0 * 4 + x1 * 2 + x0, z1 * 4 + z0 * 2 + c)


def hops(k):
    ds, dt = offset_of(k)
    ring = (0, 1, 2, 1)
    return ring[ds // 4] + ring[ds % 4] + ring[dt // 2]


def place_of(owner):
    bit = lambda b: (owner // (1 << b)) % 2
    y1, y0, x1, x0, z1, z0, c = (bit(b) for b in (6, 5, 4, 3, 2, 1, 0))
    return x1 * 64 + y1 * 32 + z1 * 16 + x0 * 8 + y0 * 4 + z0 * 2 + c


def flips(value, bits):
    parts = [(value // (1 << b)) % 2 for b in range(bits)]
    out = []
    for m in range(1 << bits):
        total = 0
        for b in range(bits):
            total = total + ((1 - parts[b]) if (m >> b) & 1 else parts[b]) * (1 << b)
        out.append(total)
    return out


def dot(a, b, dims=((1,), (0,)), precision=None):
    return lax.dot_general(a, b, (dims, ((), ())), preferred_element_type=F32, precision=precision)


def iota(shape, axis):
    return lax.broadcasted_iota(I32, shape, axis)


def mirror(points, total_t, factor, marginal):
    gradient = dot(points, total_t, ((1,), (1,))) / marginal
    row_scale = jnp.max(jnp.abs(gradient), axis=1, keepdims=True) + EPS
    tilted = factor.astype(F32) * jnp.exp(GAMMA * gradient / row_scale)
    mean = jnp.mean(tilted, axis=1, keepdims=True)
    return (tilted / jnp.where(mean > 0, mean, 1.0)).astype(BF)


def slots_of(cluster_row, me_bits):
    eye = iota((ROWS, ROWS), 0) == iota((ROWS, ROWS), 1)
    owner_row = cluster_row // CL_DEV
    cluster_col = jnp.sum(jnp.where(eye, cluster_row, 0).astype(F32), axis=1, keepdims=True).astype(I32)
    owner_col = cluster_col // CL_DEV
    same = owner_col == owner_row
    below = iota((ROWS, ROWS), 0) < iota((ROWS, ROWS), 1)
    above = iota((ROWS, ROWS), 1) < iota((ROWS, ROWS), 0)
    rank_row = jnp.sum(jnp.where(same & below, 1.0, 0.0), axis=0, keepdims=True).astype(I32)
    rank_col = jnp.sum(jnp.where(same & above, 1.0, 0.0), axis=1, keepdims=True).astype(I32)

    def block(owner):
        place = place_of(owner)
        total = 0
        for b in range(7):
            mine = me_bits[b]
            theirs = (place // (1 << b)) % 2
            total = total + (mine + theirs - 2 * mine * theirs) * (1 << b)
        return total

    return block(owner_row), rank_row, block(owner_col), rank_col, cluster_col


def kernel(
    sp_in, tp_in, sf_in, tf_in, marg, scl, tcl,
    su, tu, mp,
    sp, tp, sf, tf, pf, pp, rx, cs, rr, mm, ts, tr, ss, sr, ls, lr, tall, ball, sfall, tfall, isend, irecv,
    in_sem, pair_s, pair_r, rs_s, rs_r, ag_s, ag_r, pb_s, pb_r, tg_s, tg_r, sc_s, sc_r, rt_s, rt_r, lab_s, lab_r,
):
    s = lax.axis_index("src")
    t = lax.axis_index("tgt")
    z = t // 2
    core = t % 2
    sx = flips(s, 4)
    tx = flips(t, 3)
    zx = flips(z, 2)

    def peer(k):
        ds, dt = offset_of(k)
        return (sx[ds], tx[dt])

    partner = (s, tx[1])

    loads = [
        pltpu.make_async_copy(src, dst, in_sem.at[j])
        for j, (src, dst) in enumerate(((tp_in, tp), (tf_in, tf), (sp_in, sp), (sf_in, sf)))
    ]
    for load in loads:
        load.start()

    barrier = pltpu.get_barrier_semaphore()
    for k in sorted(range(1, NDEV), key=lambda k: -hops(k)):
        pl.semaphore_signal(barrier, inc=1, device_id=peer(k), device_id_type=MESH)

    def remote(src, dst, send, recv, device):
        return pltpu.make_async_remote_copy(
            src_ref=src, dst_ref=dst, send_sem=send, recv_sem=recv, device_id=device, device_id_type=MESH
        )

    def group_rows(g):
        return pl.ds(16, 240) if g == 0 else pl.ds(g * 256, 256)

    def group_blocks(g):
        return pl.ds(1, 15) if g == 0 else pl.ds(g * 16, 16)

    orders = [sorted((k for k in range(g * GROUP, (g + 1) * GROUP) if k), key=lambda k: -hops(k)) for g in range(NGROUP)]

    me = s * 8 + t
    my_place = place_of(me)
    me_bits = [(my_place // (1 << b)) % 2 for b in range(7)]
    s_blk_row, s_rank_row, s_blk_col, s_rank_col, s_cl_col = slots_of(scl[...], me_bits)
    t_blk_row, t_rank_row, t_blk_col, t_rank_col, t_cl_col = slots_of(tcl[...], me_bits)
    s_slot_row = s_blk_row * CAP + s_rank_row
    t_slot_row = t_blk_row * CAP + t_rank_row
    s_slot_col = s_blk_col * CAP + s_rank_col

    lane = iota((ROWS, NDEV), 1)
    blk = iota((NDEV, ROWS), 0)
    s_val = jnp.where(lane == s_rank_col, (s_cl_col % CL_DEV + 1).astype(F32), 0.0).astype(BF)
    t_val = jnp.where(lane == t_rank_col + CAP, (t_cl_col % CL_DEV + 1).astype(F32), 0.0).astype(BF)
    s_hot = jnp.where(blk == s_blk_row, 1.0, 0.0).astype(BF)
    t_hot = jnp.where(blk == t_blk_row, 1.0, 0.0).astype(BF)
    labels = (dot(s_hot, s_val) + dot(t_hot, t_val)).astype(I32)
    ls[...] = labels.reshape(NDEV, 1, NDEV)
    lr[0] = ls[0]

    loads[0].wait()
    loads[1].wait()
    part = dot(tf[...], tp[...], ((0,), (0,)))
    pf[0] = part
    pp[0] = part.astype(BF)
    loads[2].wait()
    loads[3].wait()
    part = dot(sf[...], sp[...], ((0,), (0,)))
    pf[1] = part
    pp[1] = part.astype(BF)

    row = iota((ROWS, ROWS), 0)
    col = iota((ROWS, ROWS), 1)
    to_wire = jnp.where(col == (row // 4 % 4) * 64 + (row // 16) * 4 + row % 4, 1.0, 0.0).astype(BF)
    from_wire = jnp.where(row == (col // 4 % 4) * 64 + (col // 16) * 4 + col % 4, 1.0, 0.0).astype(BF)

    def hot_rows(g, slot_row):
        return jnp.where(iota((64, ROWS), 0) + g * 64 == slot_row, 1.0, 0.0).astype(BF)

    def quarters(x):
        return jnp.concatenate([x[:, q * QUART : (q + 1) * QUART] for q in range(4)], axis=0)

    def rows_of(x):
        return jnp.concatenate([x[q * 64 : (q + 1) * 64] for q in range(4)], axis=1)

    def pack_tgt(g):
        t_sel = hot_rows(g, t_slot_row)
        s_sel = hot_rows(g, s_slot_row)
        rows = dot(t_sel, tp[...]).astype(BF)
        f_t = dot(t_sel, tf[...]).astype(BF)
        f_s = dot(s_sel, sf[...]).astype(BF)
        facs = jnp.concatenate([f_s[:, :128], f_s[:, 128:], f_t[:, :128], f_t[:, 128:]], axis=0)
        at = slice(g * 256, (g + 1) * 256)
        ts[at, 0:QUART] = dot(to_wire, quarters(rows)).astype(BF)
        ts[at, QUART : QUART + 128] = dot(to_wire, facs).astype(BF)
        if g == 0:
            tr[0:16, :] = ts[0:16, :]

    def pack_src(g):
        rows = dot(hot_rows(g, s_slot_row), sp[...]).astype(BF)
        ss[g * 256 : (g + 1) * 256, :] = dot(to_wire, quarters(rows)).astype(BF)
        if g == 0:
            sr[0:16, :] = ss[0:16, :]

    def send_tgt(g):
        for k in orders[g]:
            at = pl.ds(k * 16, 16)
            remote(ts.at[at], tr.at[at], tg_s.at[g], tg_r.at[g], peer(k)).start()
            remote(ls.at[k], lr.at[k], lab_s.at[g], lab_r.at[g], peer(k)).start()

    def send_src(g):
        for k in orders[g]:
            at = pl.ds(k * 16, 16)
            remote(ss.at[at], sr.at[at], sc_s.at[g], sc_r.at[g], peer(k)).start()

    for g in GROUPS[:PACK_EARLY]:
        pack_tgt(g)

    pl.semaphore_wait(barrier, NDEV - 1)

    pair = remote(pp.at[1 - core], rx, pair_s, pair_r, partner)
    pair.start()

    for g in GROUPS[:SENT_FIRST]:
        send_tgt(g)
    for g in GROUPS[PACK_EARLY:PACK_PAIR]:
        pack_tgt(g)

    pair.wait_recv()
    cs[...] = (pf[core] + rx[...].astype(F32)).astype(BF)

    for kc in range(1, 64):
        ds, dz = kc // 4, kc % 4
        remote(
            cs.at[pl.ds(pl.multiple_of(sx[ds] * 16, 16), 16), pl.ds(pl.multiple_of(zx[dz] * 256, 256), 256)],
            rr.at[kc], rs_s, rs_r, (sx[ds], tx[dz * 2]),
        ).start()

    for g in GROUPS[SENT_FIRST:PACK_PAIR]:
        send_tgt(g)
    for i in range(PACK_PAIR, NGROUP):
        pack_tgt(GROUPS[i])
        if i < SENT_SECOND:
            send_tgt(GROUPS[i])
    for g in GROUPS:
        pack_src(g)

    rest = rr.at[pl.ds(1, 63)]
    remote(rest, rest, rs_s, rs_r, partner).wait_recv()
    my_rows = pl.ds(pl.multiple_of(s * 16, 16), 16)
    my_cols = pl.ds(pl.multiple_of(z * 256, 256), 256)
    total = cs[my_rows, my_cols].astype(F32)
    for kc in range(1, 64):
        total = total + rr[kc].astype(F32)
    mm[core, my_rows, my_cols] = total.astype(BF)

    mine = mm.at[core, my_rows, my_cols]
    for kc in range(1, 64):
        ds, dz = kc // 4, kc % 4
        remote(mine, mine, ag_s, ag_r, (sx[ds], tx[dz * 2])).start()
    for g in GROUPS[SENT_SECOND:]:
        send_tgt(g)
    for g in GROUPS:
        send_src(g)

    def owner_tgt(g):
        at = slice(g * 256, (g + 1) * 256)
        to = slice(g * 64, (g + 1) * 64)
        remote(ts.at[group_rows(g)], tr.at[group_rows(g)], tg_s.at[g], tg_r.at[g], partner).wait_recv()
        remote(ls.at[group_blocks(g)], lr.at[group_blocks(g)], lab_s.at[g], lab_r.at[g], partner).wait_recv()
        tall[to, :] = rows_of(dot(from_wire, tr[at, 0:QUART]).astype(BF))
        facs = dot(from_wire, tr[at, QUART : QUART + 128]).astype(BF)
        sfall[to, :] = jnp.concatenate([facs[0:64], facs[64:128]], axis=1)
        tfall[to, :] = jnp.concatenate([facs[128:192], facs[192:256]], axis=1)

    for g in GROUPS[:SENT_SECOND]:
        owner_tgt(g)

    remote(rest, rest, ag_s, ag_r, partner).wait_recv()
    pair_back = remote(mm.at[core], mm.at[core], pb_s, pb_r, partner)
    pair_back.start()

    for g in GROUPS[SENT_SECOND:]:
        owner_tgt(g)

    def squares_of(points):
        total = jnp.zeros((points.shape[0], 128), F32)
        for j in range(D // 128):
            piece = points[:, j * 128 : (j + 1) * 128].astype(F32)
            total = total + piece * piece
        return total

    sums = dot(jnp.ones((8, 128), F32), squares_of(tall[...]), ((1,), (1,)), precision=lax.Precision.HIGHEST)
    inv_tgt = lax.rsqrt(sums + EPS)[0:1, :]

    got = lr[...].reshape(NDEV, NDEV).astype(F32).astype(BF)
    spread = jnp.where(iota((SLOTS, NDEV), 0) // CAP == iota((SLOTS, NDEV), 1), 1.0, 0.0).astype(BF)
    per_slot = dot(spread, got)
    slot_lane = iota((SLOTS, NDEV), 1) - iota((SLOTS, NDEV), 0) % CAP
    src_lab = jnp.sum(jnp.where(slot_lane == 0, per_slot, 0.0), axis=1, keepdims=True)
    tgt_lab = jnp.where(slot_lane == CAP, per_slot, 0.0).astype(BF)
    tgt_lab = dot(jnp.ones((8, NDEV), BF), tgt_lab, ((1,), (1,)))[0:1, :]

    remote(mm.at[1 - core], mm.at[1 - core], pb_s, pb_r, partner).wait_recv()
    marginal = marg[...]
    ball[...] = mirror(tall[...], mm[1], tfall[...], marginal)

    span = 64 * STEP

    def owner_src(groups):
        lo = min(groups)
        at0 = lo * 64
        pieces = [rows_of(dot(from_wire, sr[g * 256 : (g + 1) * 256, :]).astype(BF)) for g in sorted(groups)]
        points = jnp.concatenate(pieces, axis=0)
        update = mirror(points, mm[0], sfall[at0 : at0 + span, :], marginal)
        inv_src = lax.rsqrt(jnp.sum(squares_of(points), axis=1, keepdims=True) + EPS)
        cosine = dot(points, tall[...], ((1,), (1,))) * inv_src * inv_tgt
        weight = dot(update, ball[...], ((1,), (1,))) / R
        same = src_lab[at0 : at0 + span] == tgt_lab
        kern = jnp.where(same, weight * jnp.exp((cosine - 1.0) / TEMPER), 0.0)
        denominator = jnp.sum(kern, axis=1, keepdims=True)
        denominator = jnp.where(denominator > 0, denominator, 1.0)
        transport = (kern / denominator).astype(BF)
        image = dot(transport, tall[...]).astype(BF)
        for j, g in enumerate(sorted(groups)):
            isend[g * 256 : (g + 1) * 256, :] = dot(to_wire, quarters(image[j * 64 : (j + 1) * 64])).astype(BF)

    for first in range(0, NGROUP, STEP):
        groups = GROUPS[first : first + STEP]
        for g in groups:
            remote(ss.at[group_rows(g)], sr.at[group_rows(g)], sc_s.at[g], sc_r.at[g], partner).wait_recv()
        owner_src(groups)
        if 0 in groups:
            irecv[0:16, :] = isend[0:16, :]
        for g in groups:
            for k in orders[g]:
                at = pl.ds(k * 16, 16)
                remote(isend.at[at], irecv.at[at], rt_s.at[g], rt_r.at[g], peer(k)).start()

    su[...] = mirror(sp[...], mm[0], sf[...], marginal)
    tu[...] = mirror(tp[...], mm[1], tf[...], marginal)

    mapped = jnp.zeros((ROWS, D), F32)
    for first in range(0, NGROUP, LAST):
        groups = sorted(GROUPS[first : first + LAST])
        blocks = []
        for g in groups:
            remote(isend.at[group_rows(g)], irecv.at[group_rows(g)], rt_s.at[g], rt_r.at[g], partner).wait_recv()
            blocks.append(rows_of(dot(from_wire, irecv[g * 256 : (g + 1) * 256, :]).astype(BF)))
        images = jnp.concatenate(blocks, axis=0)
        pick = jnp.where(iota((ROWS, 64 * LAST), 1) + groups[0] * 64 == s_slot_col, 1.0, 0.0).astype(BF)
        mapped = mapped + dot(pick, images)
    mp[...] = mapped.astype(BF)

    pair.wait_send()
    remote(rest, rest, rs_s, rs_r, partner).wait_send()
    remote(rest, rest, ag_s, ag_r, partner).wait_send()
    pair_back.wait_send()
    for g in range(NGROUP):
        remote(ts.at[group_rows(g)], tr.at[group_rows(g)], tg_s.at[g], tg_r.at[g], partner).wait_send()
        remote(ls.at[group_blocks(g)], lr.at[group_blocks(g)], lab_s.at[g], lab_r.at[g], partner).wait_send()
        remote(ss.at[group_rows(g)], sr.at[group_rows(g)], sc_s.at[g], sc_r.at[g], partner).wait_send()
        remote(isend.at[group_rows(g)], irecv.at[group_rows(g)], rt_s.at[g], rt_r.at[g], partner).wait_send()


def per_device(src_points, tgt_points, src_factor, tgt_factor, inner_marginal, src_cluster, tgt_cluster):
    dma = pltpu.SemaphoreType.DMA
    vmem = pl.BlockSpec(memory_space=pltpu.VMEM)
    hbm = pl.BlockSpec(memory_space=pl.ANY)
    return pl.pallas_call(
        kernel,
        out_shape=(
            pltpu.VMEM((ROWS, R), BF),
            pltpu.VMEM((ROWS, R), BF),
            pltpu.VMEM((ROWS, D), BF),
        ),
        in_specs=[hbm] * 4 + [vmem] * 3,
        out_specs=(vmem,) * 3,
        scratch_shapes=[
            pltpu.VMEM((ROWS, D), BF),
            pltpu.VMEM((ROWS, D), BF),
            pltpu.VMEM((ROWS, R), BF),
            pltpu.VMEM((ROWS, R), BF),
            pltpu.VMEM((2, R, D), F32),
            pltpu.VMEM((2, R, D), BF),
            pltpu.VMEM((R, D), BF),
            pltpu.VMEM((R, D), BF),
            pltpu.VMEM((64, 16, 256), BF),
            pltpu.VMEM((2, R, D), BF),
            pltpu.VMEM((NDEV * 16, 384), BF),
            pltpu.VMEM((NDEV * 16, 384), BF),
            pltpu.VMEM((NDEV * 16, 256), BF),
            pltpu.VMEM((NDEV * 16, 256), BF),
            pltpu.VMEM((NDEV, 1, NDEV), I32),
            pltpu.VMEM((NDEV, 1, NDEV), I32),
            pltpu.VMEM((SLOTS, D), BF),
            pltpu.VMEM((SLOTS, R), BF),
            pltpu.VMEM((SLOTS, R), BF),
            pltpu.VMEM((SLOTS, R), BF),
            pltpu.VMEM((NDEV * 16, 256), BF),
            pltpu.VMEM((NDEV * 16, 256), BF),
        ]
        + [dma((4,))]
        + [dma] * 8
        + [dma((NGROUP,))] * 8,
        compiler_params=pltpu.CompilerParams(collective_id=0, has_side_effects=True, vmem_limit_bytes=VLIM),
        name="transport",
    )(
        src_points,
        tgt_points,
        src_factor,
        tgt_factor,
        inner_marginal.reshape(1, R),
        src_cluster.reshape(1, ROWS),
        tgt_cluster.reshape(1, ROWS),
    )


def solution(mesh):
    both = P(("src", "tgt"), None)
    flat = P(("src", "tgt"))
    return jax.shard_map(
        per_device,
        mesh=mesh,
        in_specs=(both, both, both, both, P(), flat, flat),
        out_specs=(both, both, both),
        check_vma=False,
    )
```

```python
import jax
import jax.numpy as jnp
from jax import lax
from jax.experimental import pallas as pl
from jax.experimental.pallas import tpu as pltpu
from jax.sharding import PartitionSpec as P

CL_DEV = 2
CAP = 4
GAMMA = 2.0
TEMPER = 0.03
EPS = 1e-06

D = 1024
R = 256
ROWS = 256
NDEV = 128
SLOTS = NDEV * CAP
QUART = D // 4
GROUP = 16
NGROUP = NDEV // GROUP
GROUPS = (5, 4, 7, 6, 3, 2, 1, 0)
PACK_EARLY = 2
SENT_FIRST = 2
PACK_PAIR = 4
SENT_SECOND = 8
SRC_EARLY = 0
STEP = 2
LAST = 2
VLIM = 56 << 20
MESH = pl.DeviceIdType.MESH
BF = jnp.bfloat16
F32 = jnp.float32
I32 = jnp.int32


def offset_of(k):
    g2, g1, g0, x1, x0, y1, y0 = ((k >> b) & 1 for b in (6, 5, 4, 3, 2, 1, 0))
    z1, z0, c = g2 ^ x1 ^ y1, g1 ^ x0 ^ y0, g0 ^ x0 ^ y1
    return (y1 * 8 + y0 * 4 + x1 * 2 + x0, z1 * 4 + z0 * 2 + c)


def hops(k):
    ds, dt = offset_of(k)
    ring = (0, 1, 2, 1)
    return ring[ds // 4] + ring[ds % 4] + ring[dt // 2]


def place_of(owner):
    bit = lambda b: (owner // (1 << b)) % 2
    y1, y0, x1, x0, z1, z0, c = (bit(b) for b in (6, 5, 4, 3, 2, 1, 0))
    g2, g1, g0 = (z1 + x1 + y1) % 2, (z0 + x0 + y0) % 2, (c + x0 + y1) % 2
    return g2 * 64 + g1 * 32 + g0 * 16 + x1 * 8 + x0 * 4 + y1 * 2 + y0


def flips(value, bits):
    parts = [(value // (1 << b)) % 2 for b in range(bits)]
    out = []
    for m in range(1 << bits):
        total = 0
        for b in range(bits):
            total = total + ((1 - parts[b]) if (m >> b) & 1 else parts[b]) * (1 << b)
        out.append(total)
    return out


def dot(a, b, dims=((1,), (0,)), precision=None):
    return lax.dot_general(a, b, (dims, ((), ())), preferred_element_type=F32, precision=precision)


def iota(shape, axis):
    return lax.broadcasted_iota(I32, shape, axis)


def mirror(points, total_t, factor, marginal):
    gradient = dot(points, total_t, ((1,), (1,))) / marginal
    row_scale = jnp.max(jnp.abs(gradient), axis=1, keepdims=True) + EPS
    tilted = factor.astype(F32) * jnp.exp(GAMMA * gradient / row_scale)
    mean = jnp.mean(tilted, axis=1, keepdims=True)
    return (tilted / jnp.where(mean > 0, mean, 1.0)).astype(BF)


def slots_of(cluster_row, me_bits):
    eye = iota((ROWS, ROWS), 0) == iota((ROWS, ROWS), 1)
    owner_row = cluster_row // CL_DEV
    cluster_col = jnp.sum(jnp.where(eye, cluster_row, 0).astype(F32), axis=1, keepdims=True).astype(I32)
    owner_col = cluster_col // CL_DEV
    same = owner_col == owner_row
    below = iota((ROWS, ROWS), 0) < iota((ROWS, ROWS), 1)
    above = iota((ROWS, ROWS), 1) < iota((ROWS, ROWS), 0)
    rank_row = jnp.sum(jnp.where(same & below, 1.0, 0.0), axis=0, keepdims=True).astype(I32)
    rank_col = jnp.sum(jnp.where(same & above, 1.0, 0.0), axis=1, keepdims=True).astype(I32)

    def block(owner):
        place = place_of(owner)
        total = 0
        for b in range(7):
            mine = me_bits[b]
            theirs = (place // (1 << b)) % 2
            total = total + (mine + theirs - 2 * mine * theirs) * (1 << b)
        return total

    return block(owner_row), rank_row, block(owner_col), rank_col, cluster_col


def kernel(
    sp_in, tp_in, sf_in, tf_in, marg, scl, tcl,
    su, tu, mp,
    sp, tp, sf, tf, pf, pp, rx, cs, rr, mm, ts, tr, ss, sr, ls, lr, tall, ball, sfall, tfall, isend, irecv,
    in_sem, pair_s, pair_r, rs_s, rs_r, ag_s, ag_r, pb_s, pb_r, tg_s, tg_r, sc_s, sc_r, rt_s, rt_r, lab_s, lab_r,
):
    s = lax.axis_index("src")
    t = lax.axis_index("tgt")
    z = t // 2
    core = t % 2
    sx = flips(s, 4)
    tx = flips(t, 3)
    zx = flips(z, 2)

    def peer(k):
        ds, dt = offset_of(k)
        return (sx[ds], tx[dt])

    partner = (s, tx[1])
    chips = sorted(range(1, 64), key=lambda k: ((k // 16) ^ (k // 4 % 4) ^ (k % 4), k % 4))

    loads = [
        pltpu.make_async_copy(src, dst, in_sem.at[j])
        for j, (src, dst) in enumerate(((tp_in, tp), (tf_in, tf), (sp_in, sp), (sf_in, sf)))
    ]
    for load in loads:
        load.start()

    barrier = pltpu.get_barrier_semaphore()
    for k in sorted(range(1, NDEV), key=lambda k: -hops(k)):
        pl.semaphore_signal(barrier, inc=1, device_id=peer(k), device_id_type=MESH)

    def remote(src, dst, send, recv, device):
        return pltpu.make_async_remote_copy(
            src_ref=src, dst_ref=dst, send_sem=send, recv_sem=recv, device_id=device, device_id_type=MESH
        )

    def group_rows(g):
        return pl.ds(16, 240) if g == 0 else pl.ds(g * 256, 256)

    def group_blocks(g):
        return pl.ds(1, 15) if g == 0 else pl.ds(g * 16, 16)

    orders = [sorted((k for k in range(g * GROUP, (g + 1) * GROUP) if k), key=lambda k: -hops(k)) for g in range(NGROUP)]

    me = s * 8 + t
    my_place = place_of(me)
    me_bits = [(my_place // (1 << b)) % 2 for b in range(7)]
    s_blk_row, s_rank_row, s_blk_col, s_rank_col, s_cl_col = slots_of(scl[...], me_bits)
    t_blk_row, t_rank_row, t_blk_col, t_rank_col, t_cl_col = slots_of(tcl[...], me_bits)
    s_slot_row = s_blk_row * CAP + s_rank_row
    t_slot_row = t_blk_row * CAP + t_rank_row
    s_slot_col = s_blk_col * CAP + s_rank_col

    lane = iota((ROWS, NDEV), 1)
    blk = iota((NDEV, ROWS), 0)
    s_val = jnp.where(lane == s_rank_col, (s_cl_col % CL_DEV + 1).astype(F32), 0.0).astype(BF)
    t_val = jnp.where(lane == t_rank_col + CAP, (t_cl_col % CL_DEV + 1).astype(F32), 0.0).astype(BF)
    s_hot = jnp.where(blk == s_blk_row, 1.0, 0.0).astype(BF)
    t_hot = jnp.where(blk == t_blk_row, 1.0, 0.0).astype(BF)
    labels = (dot(s_hot, s_val) + dot(t_hot, t_val)).astype(I32)
    ls[...] = labels.reshape(NDEV, 1, NDEV)
    lr[0] = ls[0]

    loads[0].wait()
    loads[1].wait()
    part = dot(tf[...], tp[...], ((0,), (0,)))
    pf[0] = part
    pp[0] = part.astype(BF)
    loads[2].wait()
    loads[3].wait()
    part = dot(sf[...], sp[...], ((0,), (0,)))
    pf[1] = part
    pp[1] = part.astype(BF)

    row = iota((ROWS, ROWS), 0)
    col = iota((ROWS, ROWS), 1)
    to_wire = jnp.where(col == (row // 4 % 4) * 64 + (row // 16) * 4 + row % 4, 1.0, 0.0).astype(BF)
    from_wire = jnp.where(row == (col // 4 % 4) * 64 + (col // 16) * 4 + col % 4, 1.0, 0.0).astype(BF)

    def hot_rows(g, slot_row):
        return jnp.where(iota((64, ROWS), 0) + g * 64 == slot_row, 1.0, 0.0).astype(BF)

    def quarters(x):
        return jnp.concatenate([x[:, q * QUART : (q + 1) * QUART] for q in range(4)], axis=0)

    def rows_of(x):
        return jnp.concatenate([x[q * 64 : (q + 1) * 64] for q in range(4)], axis=1)

    def pack_tgt(g):
        t_sel = hot_rows(g, t_slot_row)
        s_sel = hot_rows(g, s_slot_row)
        rows = dot(t_sel, tp[...]).astype(BF)
        f_t = dot(t_sel, tf[...]).astype(BF)
        f_s = dot(s_sel, sf[...]).astype(BF)
        facs = jnp.concatenate([f_s[:, :128], f_s[:, 128:], f_t[:, :128], f_t[:, 128:]], axis=0)
        at = slice(g * 256, (g + 1) * 256)
        ts[at, 0:QUART] = dot(to_wire, quarters(rows)).astype(BF)
        ts[at, QUART : QUART + 128] = dot(to_wire, facs).astype(BF)
        if g == 0:
            tr[0:16, :] = ts[0:16, :]

    def pack_src(g):
        rows = dot(hot_rows(g, s_slot_row), sp[...]).astype(BF)
        ss[g * 256 : (g + 1) * 256, :] = dot(to_wire, quarters(rows)).astype(BF)
        if g == 0:
            sr[0:16, :] = ss[0:16, :]

    def send_tgt(g):
        for k in orders[g]:
            at = pl.ds(k * 16, 16)
            remote(ts.at[at], tr.at[at], tg_s.at[g], tg_r.at[g], peer(k)).start()
            remote(ls.at[k], lr.at[k], lab_s.at[g], lab_r.at[g], peer(k)).start()

    def send_src(g):
        for k in orders[g]:
            at = pl.ds(k * 16, 16)
            remote(ss.at[at], sr.at[at], sc_s.at[g], sc_r.at[g], peer(k)).start()

    for g in GROUPS[:PACK_EARLY]:
        pack_tgt(g)

    pl.semaphore_wait(barrier, NDEV - 1)

    pair = remote(pp.at[1 - core], rx, pair_s, pair_r, partner)
    pair.start()

    for g in GROUPS[:SENT_FIRST]:
        send_tgt(g)
    for g in GROUPS[PACK_EARLY:PACK_PAIR]:
        pack_tgt(g)

    pair.wait_recv()
    cs[...] = (pf[core] + rx[...].astype(F32)).astype(BF)

    for kc in chips:
        ds, dz = kc // 4, kc % 4
        remote(
            cs.at[pl.ds(pl.multiple_of(sx[ds] * 16, 16), 16), pl.ds(pl.multiple_of(zx[dz] * 256, 256), 256)],
            rr.at[kc], rs_s, rs_r, (sx[ds], tx[dz * 2]),
        ).start()

    for g in GROUPS[SENT_FIRST:PACK_PAIR]:
        send_tgt(g)
    for i in range(PACK_PAIR, NGROUP):
        pack_tgt(GROUPS[i])
        if i < SENT_SECOND:
            send_tgt(GROUPS[i])
    for i, g in enumerate(GROUPS):
        pack_src(g)
        if i < SRC_EARLY:
            send_src(g)

    rest = rr.at[pl.ds(1, 63)]
    remote(rest, rest, rs_s, rs_r, partner).wait_recv()
    my_rows = pl.ds(pl.multiple_of(s * 16, 16), 16)
    my_cols = pl.ds(pl.multiple_of(z * 256, 256), 256)
    total = cs[my_rows, my_cols].astype(F32)
    for kc in range(1, 64):
        total = total + rr[kc].astype(F32)
    mm[core, my_rows, my_cols] = total.astype(BF)

    mine = mm.at[core, my_rows, my_cols]
    for kc in chips:
        ds, dz = kc // 4, kc % 4
        remote(mine, mine, ag_s, ag_r, (sx[ds], tx[dz * 2])).start()
    for g in GROUPS[SENT_SECOND:]:
        send_tgt(g)
    for g in GROUPS[SRC_EARLY:]:
        send_src(g)

    def owner_tgt(g):
        at = slice(g * 256, (g + 1) * 256)
        to = slice(g * 64, (g + 1) * 64)
        remote(ts.at[group_rows(g)], tr.at[group_rows(g)], tg_s.at[g], tg_r.at[g], partner).wait_recv()
        remote(ls.at[group_blocks(g)], lr.at[group_blocks(g)], lab_s.at[g], lab_r.at[g], partner).wait_recv()
        tall[to, :] = rows_of(dot(from_wire, tr[at, 0:QUART]).astype(BF))
        facs = dot(from_wire, tr[at, QUART : QUART + 128]).astype(BF)
        sfall[to, :] = jnp.concatenate([facs[0:64], facs[64:128]], axis=1)
        tfall[to, :] = jnp.concatenate([facs[128:192], facs[192:256]], axis=1)

    for g in GROUPS[:SENT_SECOND]:
        owner_tgt(g)

    remote(rest, rest, ag_s, ag_r, partner).wait_recv()
    pair_back = remote(mm.at[core], mm.at[core], pb_s, pb_r, partner)
    pair_back.start()

    for g in GROUPS[SENT_SECOND:]:
        owner_tgt(g)

    def squares_of(points):
        total = jnp.zeros((points.shape[0], 128), F32)
        for j in range(D // 128):
            piece = points[:, j * 128 : (j + 1) * 128].astype(F32)
            total = total + piece * piece
        return total

    sums = dot(jnp.ones((8, 128), F32), squares_of(tall[...]), ((1,), (1,)), precision=lax.Precision.HIGHEST)
    inv_tgt = lax.rsqrt(sums + EPS)[0:1, :]

    got = lr[...].reshape(NDEV, NDEV).astype(F32).astype(BF)
    spread = jnp.where(iota((SLOTS, NDEV), 0) // CAP == iota((SLOTS, NDEV), 1), 1.0, 0.0).astype(BF)
    per_slot = dot(spread, got)
    slot_lane = iota((SLOTS, NDEV), 1) - iota((SLOTS, NDEV), 0) % CAP
    src_lab = jnp.sum(jnp.where(slot_lane == 0, per_slot, 0.0), axis=1, keepdims=True)
    tgt_lab = jnp.where(slot_lane == CAP, per_slot, 0.0).astype(BF)
    tgt_lab = dot(jnp.ones((8, NDEV), BF), tgt_lab, ((1,), (1,)))[0:1, :]

    remote(mm.at[1 - core], mm.at[1 - core], pb_s, pb_r, partner).wait_recv()
    marginal = marg[...]
    ball[...] = mirror(tall[...], mm[1], tfall[...], marginal)

    span = 64 * STEP

    def owner_src(groups):
        lo = min(groups)
        at0 = lo * 64
        pieces = [rows_of(dot(from_wire, sr[g * 256 : (g + 1) * 256, :]).astype(BF)) for g in sorted(groups)]
        points = jnp.concatenate(pieces, axis=0)
        update = mirror(points, mm[0], sfall[at0 : at0 + span, :], marginal)
        inv_src = lax.rsqrt(jnp.sum(squares_of(points), axis=1, keepdims=True) + EPS)
        cosine = dot(points, tall[...], ((1,), (1,))) * inv_src * inv_tgt
        weight = dot(update, ball[...], ((1,), (1,))) / R
        same = src_lab[at0 : at0 + span] == tgt_lab
        kern = jnp.where(same, weight * jnp.exp((cosine - 1.0) / TEMPER), 0.0)
        denominator = jnp.sum(kern, axis=1, keepdims=True)
        denominator = jnp.where(denominator > 0, denominator, 1.0)
        transport = (kern / denominator).astype(BF)
        image = dot(transport, tall[...]).astype(BF)
        for j, g in enumerate(sorted(groups)):
            isend[g * 256 : (g + 1) * 256, :] = dot(to_wire, quarters(image[j * 64 : (j + 1) * 64])).astype(BF)

    for first in range(0, NGROUP, STEP):
        groups = GROUPS[first : first + STEP]
        for g in groups:
            remote(ss.at[group_rows(g)], sr.at[group_rows(g)], sc_s.at[g], sc_r.at[g], partner).wait_recv()
        owner_src(groups)
        if 0 in groups:
            irecv[0:16, :] = isend[0:16, :]
        for g in groups:
            for k in orders[g]:
                at = pl.ds(k * 16, 16)
                remote(isend.at[at], irecv.at[at], rt_s.at[g], rt_r.at[g], peer(k)).start()

    su[...] = mirror(sp[...], mm[0], sf[...], marginal)
    tu[...] = mirror(tp[...], mm[1], tf[...], marginal)

    mapped = jnp.zeros((ROWS, D), F32)
    for first in range(0, NGROUP, LAST):
        groups = sorted(GROUPS[first : first + LAST])
        blocks = []
        for g in groups:
            remote(isend.at[group_rows(g)], irecv.at[group_rows(g)], rt_s.at[g], rt_r.at[g], partner).wait_recv()
            blocks.append(rows_of(dot(from_wire, irecv[g * 256 : (g + 1) * 256, :]).astype(BF)))
        images = jnp.concatenate(blocks, axis=0)
        pick = jnp.where(iota((ROWS, 64 * LAST), 1) + groups[0] * 64 == s_slot_col, 1.0, 0.0).astype(BF)
        mapped = mapped + dot(pick, images)
    mp[...] = mapped.astype(BF)

    pair.wait_send()
    remote(rest, rest, rs_s, rs_r, partner).wait_send()
    remote(rest, rest, ag_s, ag_r, partner).wait_send()
    pair_back.wait_send()
    for g in range(NGROUP):
        remote(ts.at[group_rows(g)], tr.at[group_rows(g)], tg_s.at[g], tg_r.at[g], partner).wait_send()
        remote(ls.at[group_blocks(g)], lr.at[group_blocks(g)], lab_s.at[g], lab_r.at[g], partner).wait_send()
        remote(ss.at[group_rows(g)], sr.at[group_rows(g)], sc_s.at[g], sc_r.at[g], partner).wait_send()
        remote(isend.at[group_rows(g)], irecv.at[group_rows(g)], rt_s.at[g], rt_r.at[g], partner).wait_send()


def put_out(su, tu, mp, su_out, tu_out, mp_out, sems):
    copies = [
        pltpu.make_async_copy(src, dst, sems.at[j])
        for j, (src, dst) in enumerate(((mp, mp_out), (su, su_out), (tu, tu_out)))
    ]
    for copy in copies:
        copy.start()
    for copy in copies:
        copy.wait()


def per_device(src_points, tgt_points, src_factor, tgt_factor, inner_marginal, src_cluster, tgt_cluster):
    dma = pltpu.SemaphoreType.DMA
    vmem = pl.BlockSpec(memory_space=pltpu.VMEM)
    hbm = pl.BlockSpec(memory_space=pl.ANY)
    su, tu, mp = pl.pallas_call(
        kernel,
        out_shape=(
            pltpu.VMEM((ROWS, R), BF),
            pltpu.VMEM((ROWS, R), BF),
            pltpu.VMEM((ROWS, D), BF),
        ),
        in_specs=[hbm] * 4 + [vmem] * 3,
        out_specs=(vmem,) * 3,
        scratch_shapes=[
            pltpu.VMEM((ROWS, D), BF),
            pltpu.VMEM((ROWS, D), BF),
            pltpu.VMEM((ROWS, R), BF),
            pltpu.VMEM((ROWS, R), BF),
            pltpu.VMEM((2, R, D), F32),
            pltpu.VMEM((2, R, D), BF),
            pltpu.VMEM((R, D), BF),
            pltpu.VMEM((R, D), BF),
            pltpu.VMEM((64, 16, 256), BF),
            pltpu.VMEM((2, R, D), BF),
            pltpu.VMEM((NDEV * 16, 384), BF),
            pltpu.VMEM((NDEV * 16, 384), BF),
            pltpu.VMEM((NDEV * 16, 256), BF),
            pltpu.VMEM((NDEV * 16, 256), BF),
            pltpu.VMEM((NDEV, 1, NDEV), I32),
            pltpu.VMEM((NDEV, 1, NDEV), I32),
            pltpu.VMEM((SLOTS, D), BF),
            pltpu.VMEM((SLOTS, R), BF),
            pltpu.VMEM((SLOTS, R), BF),
            pltpu.VMEM((SLOTS, R), BF),
            pltpu.VMEM((NDEV * 16, 256), BF),
            pltpu.VMEM((NDEV * 16, 256), BF),
        ]
        + [dma((4,))]
        + [dma] * 8
        + [dma((NGROUP,))] * 8,
        compiler_params=pltpu.CompilerParams(collective_id=0, has_side_effects=True, vmem_limit_bytes=VLIM),
        name="transport",
    )(
        src_points,
        tgt_points,
        src_factor,
        tgt_factor,
        inner_marginal.reshape(1, R),
        src_cluster.reshape(1, ROWS),
        tgt_cluster.reshape(1, ROWS),
    )
    shape = jax.ShapeDtypeStruct
    return pl.pallas_call(
        put_out,
        out_shape=(shape((ROWS, R), BF), shape((ROWS, R), BF), shape((ROWS, D), BF)),
        in_specs=[vmem] * 3,
        out_specs=(hbm,) * 3,
        scratch_shapes=[dma((3,))],
        name="put_out",
    )(*(pltpu.with_memory_space_constraint(x, pltpu.VMEM) for x in (su, tu, mp)))


def solution(mesh):
    both = P(("src", "tgt"), None)
    flat = P(("src", "tgt"))
    return jax.shard_map(
        per_device,
        mesh=mesh,
        in_specs=(both, both, both, both, P(), flat, flat),
        out_specs=(both, both, both),
        check_vma=False,
    )
```

```python
import jax
import jax.numpy as jnp
from jax import lax
from jax.experimental import pallas as pl
from jax.experimental.pallas import tpu as pltpu
from jax.sharding import PartitionSpec as P

CL_DEV = 2
CAP = 4
GAMMA = 2.0
TEMPER = 0.03
EPS = 1e-06

D = 1024
R = 256
ROWS = 256
NDEV = 128
SLOTS = NDEV * CAP
QUART = D // 4
GROUP = 16
NGROUP = NDEV // GROUP
GROUPS = (5, 4, 7, 6, 3, 2, 1, 0)
PACK_EARLY = 2
SENT_FIRST = 2
PACK_PAIR = 4
SENT_SECOND = 8
SRC_EARLY = 0
STEP = 2
LAST = 2
VLIM = 56 << 20
MESH = pl.DeviceIdType.MESH
BF = jnp.bfloat16
F32 = jnp.float32
I32 = jnp.int32


def offset_of(k):
    g2, g1, g0, x1, x0, y1, y0 = ((k >> b) & 1 for b in (6, 5, 4, 3, 2, 1, 0))
    z1, z0, c = g2 ^ x1 ^ y1, g1 ^ x0 ^ y0, g0 ^ x0 ^ y1
    return (y1 * 8 + y0 * 4 + x1 * 2 + x0, z1 * 4 + z0 * 2 + c)


def hops(k):
    ds, dt = offset_of(k)
    ring = (0, 1, 2, 1)
    return ring[ds // 4] + ring[ds % 4] + ring[dt // 2]


def place_of(owner):
    bit = lambda b: (owner // (1 << b)) % 2
    y1, y0, x1, x0, z1, z0, c = (bit(b) for b in (6, 5, 4, 3, 2, 1, 0))
    g2, g1, g0 = (z1 + x1 + y1) % 2, (z0 + x0 + y0) % 2, (c + x0 + y1) % 2
    return g2 * 64 + g1 * 32 + g0 * 16 + x1 * 8 + x0 * 4 + y1 * 2 + y0


def flips(value, bits):
    parts = [(value // (1 << b)) % 2 for b in range(bits)]
    out = []
    for m in range(1 << bits):
        total = 0
        for b in range(bits):
            total = total + ((1 - parts[b]) if (m >> b) & 1 else parts[b]) * (1 << b)
        out.append(total)
    return out


def dot(a, b, dims=((1,), (0,)), precision=None):
    return lax.dot_general(a, b, (dims, ((), ())), preferred_element_type=F32, precision=precision)


def iota(shape, axis):
    return lax.broadcasted_iota(I32, shape, axis)


def mirror(points, total_t, factor, marginal):
    gradient = dot(points, total_t, ((1,), (1,))) / marginal
    row_scale = jnp.max(jnp.abs(gradient), axis=1, keepdims=True) + EPS
    tilted = factor.astype(F32) * jnp.exp(GAMMA * gradient / row_scale)
    mean = jnp.mean(tilted, axis=1, keepdims=True)
    return (tilted / jnp.where(mean > 0, mean, 1.0)).astype(BF)


def slots_of(cluster_row, me_bits):
    eye = iota((ROWS, ROWS), 0) == iota((ROWS, ROWS), 1)
    owner_row = cluster_row // CL_DEV
    cluster_col = jnp.sum(jnp.where(eye, cluster_row, 0).astype(F32), axis=1, keepdims=True).astype(I32)
    owner_col = cluster_col // CL_DEV
    same = owner_col == owner_row
    below = iota((ROWS, ROWS), 0) < iota((ROWS, ROWS), 1)
    above = iota((ROWS, ROWS), 1) < iota((ROWS, ROWS), 0)
    rank_row = jnp.sum(jnp.where(same & below, 1.0, 0.0), axis=0, keepdims=True).astype(I32)
    rank_col = jnp.sum(jnp.where(same & above, 1.0, 0.0), axis=1, keepdims=True).astype(I32)

    def block(owner):
        place = place_of(owner)
        total = 0
        for b in range(7):
            mine = me_bits[b]
            theirs = (place // (1 << b)) % 2
            total = total + (mine + theirs - 2 * mine * theirs) * (1 << b)
        return total

    return block(owner_row), rank_row, block(owner_col), rank_col, cluster_col


def kernel(
    sp_in, tp_in, sf_in, tf_in, marg, scl, tcl,
    su, tu, mp,
    sp, tp, sf, tf, pf, pp, rx, cs, rr, mm, ts, tr, ss, sr, ls, lr, tall, ball, sfall, tfall, isend, irecv,
    in_sem, pair_s, pair_r, rs_s, rs_r, ag_s, ag_r, pb_s, pb_r, tg_s, tg_r, sc_s, sc_r, rt_s, rt_r, lab_s, lab_r,
):
    s = lax.axis_index("src")
    t = lax.axis_index("tgt")
    z = t // 2
    core = t % 2
    sx = flips(s, 4)
    tx = flips(t, 3)
    zx = flips(z, 2)

    def peer(k):
        ds, dt = offset_of(k)
        return (sx[ds], tx[dt])

    partner = (s, tx[1])
    chips = sorted(range(1, 64), key=lambda k: -((0, 1, 2, 1)[k // 16] + (0, 1, 2, 1)[k // 4 % 4] + (0, 1, 2, 1)[k % 4]))

    loads = [
        pltpu.make_async_copy(src, dst, in_sem.at[j])
        for j, (src, dst) in enumerate(((tp_in, tp), (tf_in, tf), (sp_in, sp), (sf_in, sf)))
    ]
    for load in loads:
        load.start()

    barrier = pltpu.get_barrier_semaphore()
    for k in sorted(range(1, NDEV), key=lambda k: -hops(k)):
        pl.semaphore_signal(barrier, inc=1, device_id=peer(k), device_id_type=MESH)

    def remote(src, dst, send, recv, device):
        return pltpu.make_async_remote_copy(
            src_ref=src, dst_ref=dst, send_sem=send, recv_sem=recv, device_id=device, device_id_type=MESH
        )

    def group_rows(g):
        return pl.ds(16, 240) if g == 0 else pl.ds(g * 256, 256)

    def group_blocks(g):
        return pl.ds(1, 15) if g == 0 else pl.ds(g * 16, 16)

    orders = [sorted((k for k in range(g * GROUP, (g + 1) * GROUP) if k), key=lambda k: -hops(k)) for g in range(NGROUP)]

    me = s * 8 + t
    my_place = place_of(me)
    me_bits = [(my_place // (1 << b)) % 2 for b in range(7)]
    s_blk_row, s_rank_row, s_blk_col, s_rank_col, s_cl_col = slots_of(scl[...], me_bits)
    t_blk_row, t_rank_row, t_blk_col, t_rank_col, t_cl_col = slots_of(tcl[...], me_bits)
    s_slot_row = s_blk_row * CAP + s_rank_row
    t_slot_row = t_blk_row * CAP + t_rank_row
    s_slot_col = s_blk_col * CAP + s_rank_col

    lane = iota((ROWS, NDEV), 1)
    blk = iota((NDEV, ROWS), 0)
    s_val = jnp.where(lane == s_rank_col, (s_cl_col % CL_DEV + 1).astype(F32), 0.0).astype(BF)
    t_val = jnp.where(lane == t_rank_col + CAP, (t_cl_col % CL_DEV + 1).astype(F32), 0.0).astype(BF)
    s_hot = jnp.where(blk == s_blk_row, 1.0, 0.0).astype(BF)
    t_hot = jnp.where(blk == t_blk_row, 1.0, 0.0).astype(BF)
    labels = (dot(s_hot, s_val) + dot(t_hot, t_val)).astype(I32)
    ls[...] = labels.reshape(NDEV, 1, NDEV)
    lr[0] = ls[0]

    loads[0].wait()
    loads[1].wait()
    part = dot(tf[...], tp[...], ((0,), (0,)))
    pf[0] = part
    pp[0] = part.astype(BF)
    loads[2].wait()
    loads[3].wait()
    part = dot(sf[...], sp[...], ((0,), (0,)))
    pf[1] = part
    pp[1] = part.astype(BF)

    row = iota((ROWS, ROWS), 0)
    col = iota((ROWS, ROWS), 1)
    to_wire = jnp.where(col == (row // 4 % 4) * 64 + (row // 16) * 4 + row % 4, 1.0, 0.0).astype(BF)
    from_wire = jnp.where(row == (col // 4 % 4) * 64 + (col // 16) * 4 + col % 4, 1.0, 0.0).astype(BF)

    def hot_rows(g, slot_row):
        return jnp.where(iota((64, ROWS), 0) + g * 64 == slot_row, 1.0, 0.0).astype(BF)

    def quarters(x):
        return jnp.concatenate([x[:, q * QUART : (q + 1) * QUART] for q in range(4)], axis=0)

    def rows_of(x):
        return jnp.concatenate([x[q * 64 : (q + 1) * 64] for q in range(4)], axis=1)

    def pack_tgt(g):
        t_sel = hot_rows(g, t_slot_row)
        s_sel = hot_rows(g, s_slot_row)
        rows = dot(t_sel, tp[...]).astype(BF)
        f_t = dot(t_sel, tf[...]).astype(BF)
        f_s = dot(s_sel, sf[...]).astype(BF)
        facs = jnp.concatenate([f_s[:, :128], f_s[:, 128:], f_t[:, :128], f_t[:, 128:]], axis=0)
        at = slice(g * 256, (g + 1) * 256)
        ts[at, 0:QUART] = dot(to_wire, quarters(rows)).astype(BF)
        ts[at, QUART : QUART + 128] = dot(to_wire, facs).astype(BF)
        if g == 0:
            tr[0:16, :] = ts[0:16, :]

    def pack_src(g):
        rows = dot(hot_rows(g, s_slot_row), sp[...]).astype(BF)
        ss[g * 256 : (g + 1) * 256, :] = dot(to_wire, quarters(rows)).astype(BF)
        if g == 0:
            sr[0:16, :] = ss[0:16, :]

    def send_tgt(g):
        for k in orders[g]:
            at = pl.ds(k * 16, 16)
            remote(ts.at[at], tr.at[at], tg_s.at[g], tg_r.at[g], peer(k)).start()
            remote(ls.at[k], lr.at[k], lab_s.at[g], lab_r.at[g], peer(k)).start()

    def send_src(g):
        for k in orders[g]:
            at = pl.ds(k * 16, 16)
            remote(ss.at[at], sr.at[at], sc_s.at[g], sc_r.at[g], peer(k)).start()

    for g in GROUPS[:PACK_EARLY]:
        pack_tgt(g)

    pl.semaphore_wait(barrier, NDEV - 1)

    pair = remote(pp.at[1 - core], rx, pair_s, pair_r, partner)
    pair.start()

    for g in GROUPS[:SENT_FIRST]:
        send_tgt(g)
    for g in GROUPS[PACK_EARLY:PACK_PAIR]:
        pack_tgt(g)

    pair.wait_recv()
    cs[...] = (pf[core] + rx[...].astype(F32)).astype(BF)

    for kc in chips:
        ds, dz = kc // 4, kc % 4
        remote(
            cs.at[pl.ds(pl.multiple_of(sx[ds] * 16, 16), 16), pl.ds(pl.multiple_of(zx[dz] * 256, 256), 256)],
            rr.at[kc], rs_s, rs_r, (sx[ds], tx[dz * 2]),
        ).start()

    for g in GROUPS[SENT_FIRST:PACK_PAIR]:
        send_tgt(g)
    for i in range(PACK_PAIR, NGROUP):
        pack_tgt(GROUPS[i])
        if i < SENT_SECOND:
            send_tgt(GROUPS[i])
    for i, g in enumerate(GROUPS):
        pack_src(g)
        if i < SRC_EARLY:
            send_src(g)

    rest = rr.at[pl.ds(1, 63)]
    remote(rest, rest, rs_s, rs_r, partner).wait_recv()
    my_rows = pl.ds(pl.multiple_of(s * 16, 16), 16)
    my_cols = pl.ds(pl.multiple_of(z * 256, 256), 256)
    total = cs[my_rows, my_cols].astype(F32)
    for kc in range(1, 64):
        total = total + rr[kc].astype(F32)
    mm[core, my_rows, my_cols] = total.astype(BF)

    mine = mm.at[core, my_rows, my_cols]
    for kc in chips:
        ds, dz = kc // 4, kc % 4
        remote(mine, mine, ag_s, ag_r, (sx[ds], tx[dz * 2])).start()
    for g in GROUPS[SENT_SECOND:]:
        send_tgt(g)
    for g in GROUPS[SRC_EARLY:]:
        send_src(g)

    def owner_tgt(g):
        at = slice(g * 256, (g + 1) * 256)
        to = slice(g * 64, (g + 1) * 64)
        remote(ts.at[group_rows(g)], tr.at[group_rows(g)], tg_s.at[g], tg_r.at[g], partner).wait_recv()
        remote(ls.at[group_blocks(g)], lr.at[group_blocks(g)], lab_s.at[g], lab_r.at[g], partner).wait_recv()
        tall[to, :] = rows_of(dot(from_wire, tr[at, 0:QUART]).astype(BF))
        facs = dot(from_wire, tr[at, QUART : QUART + 128]).astype(BF)
        sfall[to, :] = jnp.concatenate([facs[0:64], facs[64:128]], axis=1)
        tfall[to, :] = jnp.concatenate([facs[128:192], facs[192:256]], axis=1)

    for g in GROUPS[:SENT_SECOND]:
        owner_tgt(g)

    remote(rest, rest, ag_s, ag_r, partner).wait_recv()
    pair_back = remote(mm.at[core], mm.at[core], pb_s, pb_r, partner)
    pair_back.start()

    for g in GROUPS[SENT_SECOND:]:
        owner_tgt(g)

    def squares_of(points):
        total = jnp.zeros((points.shape[0], 128), F32)
        for j in range(D // 128):
            piece = points[:, j * 128 : (j + 1) * 128].astype(F32)
            total = total + piece * piece
        return total

    sums = dot(jnp.ones((8, 128), F32), squares_of(tall[...]), ((1,), (1,)), precision=lax.Precision.HIGHEST)
    inv_tgt = lax.rsqrt(sums + EPS)[0:1, :]

    got = lr[...].reshape(NDEV, NDEV).astype(F32).astype(BF)
    spread = jnp.where(iota((SLOTS, NDEV), 0) // CAP == iota((SLOTS, NDEV), 1), 1.0, 0.0).astype(BF)
    per_slot = dot(spread, got)
    slot_lane = iota((SLOTS, NDEV), 1) - iota((SLOTS, NDEV), 0) % CAP
    src_lab = jnp.sum(jnp.where(slot_lane == 0, per_slot, 0.0), axis=1, keepdims=True)
    tgt_lab = jnp.where(slot_lane == CAP, per_slot, 0.0).astype(BF)
    tgt_lab = dot(jnp.ones((8, NDEV), BF), tgt_lab, ((1,), (1,)))[0:1, :]

    remote(mm.at[1 - core], mm.at[1 - core], pb_s, pb_r, partner).wait_recv()
    marginal = marg[...]
    ball[...] = mirror(tall[...], mm[1], tfall[...], marginal)

    span = 64 * STEP

    def owner_src(groups):
        lo = min(groups)
        at0 = lo * 64
        pieces = [rows_of(dot(from_wire, sr[g * 256 : (g + 1) * 256, :]).astype(BF)) for g in sorted(groups)]
        points = jnp.concatenate(pieces, axis=0)
        update = mirror(points, mm[0], sfall[at0 : at0 + span, :], marginal)
        inv_src = lax.rsqrt(jnp.sum(squares_of(points), axis=1, keepdims=True) + EPS)
        cosine = dot(points, tall[...], ((1,), (1,))) * inv_src * inv_tgt
        weight = dot(update, ball[...], ((1,), (1,))) / R
        same = src_lab[at0 : at0 + span] == tgt_lab
        kern = jnp.where(same, weight * jnp.exp((cosine - 1.0) / TEMPER), 0.0)
        denominator = jnp.sum(kern, axis=1, keepdims=True)
        denominator = jnp.where(denominator > 0, denominator, 1.0)
        transport = (kern / denominator).astype(BF)
        image = dot(transport, tall[...]).astype(BF)
        for j, g in enumerate(sorted(groups)):
            isend[g * 256 : (g + 1) * 256, :] = dot(to_wire, quarters(image[j * 64 : (j + 1) * 64])).astype(BF)

    for first in range(0, NGROUP, STEP):
        groups = GROUPS[first : first + STEP]
        for g in groups:
            remote(ss.at[group_rows(g)], sr.at[group_rows(g)], sc_s.at[g], sc_r.at[g], partner).wait_recv()
        owner_src(groups)
        if 0 in groups:
            irecv[0:16, :] = isend[0:16, :]
        for g in groups:
            for k in orders[g]:
                at = pl.ds(k * 16, 16)
                remote(isend.at[at], irecv.at[at], rt_s.at[g], rt_r.at[g], peer(k)).start()

    su[...] = mirror(sp[...], mm[0], sf[...], marginal)
    tu[...] = mirror(tp[...], mm[1], tf[...], marginal)

    mapped = jnp.zeros((ROWS, D), F32)
    for first in range(0, NGROUP, LAST):
        groups = sorted(GROUPS[first : first + LAST])
        blocks = []
        for g in groups:
            remote(isend.at[group_rows(g)], irecv.at[group_rows(g)], rt_s.at[g], rt_r.at[g], partner).wait_recv()
            blocks.append(rows_of(dot(from_wire, irecv[g * 256 : (g + 1) * 256, :]).astype(BF)))
        images = jnp.concatenate(blocks, axis=0)
        pick = jnp.where(iota((ROWS, 64 * LAST), 1) + groups[0] * 64 == s_slot_col, 1.0, 0.0).astype(BF)
        mapped = mapped + dot(pick, images)
    mp[...] = mapped.astype(BF)

    pair.wait_send()
    remote(rest, rest, rs_s, rs_r, partner).wait_send()
    remote(rest, rest, ag_s, ag_r, partner).wait_send()
    pair_back.wait_send()
    for g in range(NGROUP):
        remote(ts.at[group_rows(g)], tr.at[group_rows(g)], tg_s.at[g], tg_r.at[g], partner).wait_send()
        remote(ls.at[group_blocks(g)], lr.at[group_blocks(g)], lab_s.at[g], lab_r.at[g], partner).wait_send()
        remote(ss.at[group_rows(g)], sr.at[group_rows(g)], sc_s.at[g], sc_r.at[g], partner).wait_send()
        remote(isend.at[group_rows(g)], irecv.at[group_rows(g)], rt_s.at[g], rt_r.at[g], partner).wait_send()


def put_out(su, tu, mp, su_out, tu_out, mp_out, sems):
    copies = [
        pltpu.make_async_copy(src, dst, sems.at[j])
        for j, (src, dst) in enumerate(((mp, mp_out), (su, su_out), (tu, tu_out)))
    ]
    for copy in copies:
        copy.start()
    for copy in copies:
        copy.wait()


def per_device(src_points, tgt_points, src_factor, tgt_factor, inner_marginal, src_cluster, tgt_cluster):
    dma = pltpu.SemaphoreType.DMA
    vmem = pl.BlockSpec(memory_space=pltpu.VMEM)
    hbm = pl.BlockSpec(memory_space=pl.ANY)
    su, tu, mp = pl.pallas_call(
        kernel,
        out_shape=(
            pltpu.VMEM((ROWS, R), BF),
            pltpu.VMEM((ROWS, R), BF),
            pltpu.VMEM((ROWS, D), BF),
        ),
        in_specs=[hbm] * 4 + [vmem] * 3,
        out_specs=(vmem,) * 3,
        scratch_shapes=[
            pltpu.VMEM((ROWS, D), BF),
            pltpu.VMEM((ROWS, D), BF),
            pltpu.VMEM((ROWS, R), BF),
            pltpu.VMEM((ROWS, R), BF),
            pltpu.VMEM((2, R, D), F32),
            pltpu.VMEM((2, R, D), BF),
            pltpu.VMEM((R, D), BF),
            pltpu.VMEM((R, D), BF),
            pltpu.VMEM((64, 16, 256), BF),
            pltpu.VMEM((2, R, D), BF),
            pltpu.VMEM((NDEV * 16, 384), BF),
            pltpu.VMEM((NDEV * 16, 384), BF),
            pltpu.VMEM((NDEV * 16, 256), BF),
            pltpu.VMEM((NDEV * 16, 256), BF),
            pltpu.VMEM((NDEV, 1, NDEV), I32),
            pltpu.VMEM((NDEV, 1, NDEV), I32),
            pltpu.VMEM((SLOTS, D), BF),
            pltpu.VMEM((SLOTS, R), BF),
            pltpu.VMEM((SLOTS, R), BF),
            pltpu.VMEM((SLOTS, R), BF),
            pltpu.VMEM((NDEV * 16, 256), BF),
            pltpu.VMEM((NDEV * 16, 256), BF),
        ]
        + [dma((4,))]
        + [dma] * 8
        + [dma((NGROUP,))] * 8,
        compiler_params=pltpu.CompilerParams(collective_id=0, has_side_effects=True, vmem_limit_bytes=VLIM),
        name="transport",
    )(
        src_points,
        tgt_points,
        src_factor,
        tgt_factor,
        inner_marginal.reshape(1, R),
        src_cluster.reshape(1, ROWS),
        tgt_cluster.reshape(1, ROWS),
    )
    shape = jax.ShapeDtypeStruct
    return pl.pallas_call(
        put_out,
        out_shape=(shape((ROWS, R), BF), shape((ROWS, R), BF), shape((ROWS, D), BF)),
        in_specs=[vmem] * 3,
        out_specs=(hbm,) * 3,
        scratch_shapes=[dma((3,))],
        name="put_out",
    )(*(pltpu.with_memory_space_constraint(x, pltpu.VMEM) for x in (su, tu, mp)))


def solution(mesh):
    both = P(("src", "tgt"), None)
    flat = P(("src", "tgt"))
    return jax.shard_map(
        per_device,
        mesh=mesh,
        in_specs=(both, both, both, both, P(), flat, flat),
        out_specs=(both, both, both),
        check_vma=False,
    )
```

```python
import jax
import jax.numpy as jnp
from jax import lax
from jax.experimental import pallas as pl
from jax.experimental.pallas import tpu as pltpu
from jax.sharding import PartitionSpec as P

CL_DEV = 2
CAP = 4
GAMMA = 2.0
TEMPER = 0.03
EPS = 1e-06

D = 1024
R = 256
ROWS = 256
NDEV = 128
SLOTS = NDEV * CAP
QUART = D // 4
GROUP = 16
NGROUP = NDEV // GROUP
GROUPS = (5, 4, 7, 6, 3, 2, 1, 0)
PACK_EARLY = 2
SENT_FIRST = 2
PACK_PAIR = 4
SRC_NOW = 4
SRC_MID = 8
MID_AT = 7
STEP = 2
LAST = 2
VLIM = 56 << 20
MESH = pl.DeviceIdType.MESH
BF = jnp.bfloat16
F32 = jnp.float32
I32 = jnp.int32


def offset_of(k):
    g2, g1, g0, x1, x0, y1, y0 = ((k >> b) & 1 for b in (6, 5, 4, 3, 2, 1, 0))
    z1, z0, c = g2 ^ x1 ^ y1, g1 ^ x0 ^ y0, g0 ^ x0 ^ y1
    return (y1 * 8 + y0 * 4 + x1 * 2 + x0, z1 * 4 + z0 * 2 + c)


def hops(k):
    ds, dt = offset_of(k)
    ring = (0, 1, 2, 1)
    return ring[ds // 4] + ring[ds % 4] + ring[dt // 2]


def place_of(owner):
    bit = lambda b: (owner // (1 << b)) % 2
    y1, y0, x1, x0, z1, z0, c = (bit(b) for b in (6, 5, 4, 3, 2, 1, 0))
    g2, g1, g0 = (z1 + x1 + y1) % 2, (z0 + x0 + y0) % 2, (c + x0 + y1) % 2
    return g2 * 64 + g1 * 32 + g0 * 16 + x1 * 8 + x0 * 4 + y1 * 2 + y0


def flips(value, bits):
    parts = [(value // (1 << b)) % 2 for b in range(bits)]
    out = []
    for m in range(1 << bits):
        total = 0
        for b in range(bits):
            total = total + ((1 - parts[b]) if (m >> b) & 1 else parts[b]) * (1 << b)
        out.append(total)
    return out


def dot(a, b, dims=((1,), (0,)), precision=None):
    return lax.dot_general(a, b, (dims, ((), ())), preferred_element_type=F32, precision=precision)


def iota(shape, axis):
    return lax.broadcasted_iota(I32, shape, axis)


def mirror(points, total_t, factor, marginal):
    gradient = dot(points, total_t, ((1,), (1,))) / marginal
    row_scale = jnp.max(jnp.abs(gradient), axis=1, keepdims=True) + EPS
    tilted = factor.astype(F32) * jnp.exp(GAMMA * gradient / row_scale)
    mean = jnp.mean(tilted, axis=1, keepdims=True)
    return (tilted / jnp.where(mean > 0, mean, 1.0)).astype(BF)


def slots_of(cluster_row, me_bits):
    eye = iota((ROWS, ROWS), 0) == iota((ROWS, ROWS), 1)
    owner_row = cluster_row // CL_DEV
    cluster_col = jnp.sum(jnp.where(eye, cluster_row, 0).astype(F32), axis=1, keepdims=True).astype(I32)
    owner_col = cluster_col // CL_DEV
    same = owner_col == owner_row
    below = iota((ROWS, ROWS), 0) < iota((ROWS, ROWS), 1)
    above = iota((ROWS, ROWS), 1) < iota((ROWS, ROWS), 0)
    rank_row = jnp.sum(jnp.where(same & below, 1.0, 0.0), axis=0, keepdims=True).astype(I32)
    rank_col = jnp.sum(jnp.where(same & above, 1.0, 0.0), axis=1, keepdims=True).astype(I32)

    def block(owner):
        place = place_of(owner)
        total = 0
        for b in range(7):
            mine = me_bits[b]
            theirs = (place // (1 << b)) % 2
            total = total + (mine + theirs - 2 * mine * theirs) * (1 << b)
        return total

    return block(owner_row), rank_row, block(owner_col), rank_col, cluster_col


def kernel(
    sp_in, tp_in, sf_in, tf_in, marg, scl, tcl,
    su, tu, mp,
    sp, tp, sf, tf, pf, pp, rx, cs, rr, mm, ts, tr, ss, sr, ls, lr, tall, ball, sfall, tfall, isend, irecv,
    in_sem, pair_s, pair_r, rs_s, rs_r, ag_s, ag_r, pb_s, pb_r, tg_s, tg_r, sc_s, sc_r, rt_s, rt_r, lab_s, lab_r,
):
    s = lax.axis_index("src")
    t = lax.axis_index("tgt")
    z = t // 2
    core = t % 2
    sx = flips(s, 4)
    tx = flips(t, 3)
    zx = flips(z, 2)

    def peer(k):
        ds, dt = offset_of(k)
        return (sx[ds], tx[dt])

    partner = (s, tx[1])
    chips = sorted(range(1, 64), key=lambda k: -((0, 1, 2, 1)[k // 16] + (0, 1, 2, 1)[k // 4 % 4] + (0, 1, 2, 1)[k % 4]))

    loads = [
        pltpu.make_async_copy(src, dst, in_sem.at[j])
        for j, (src, dst) in enumerate(((tp_in, tp), (tf_in, tf), (sp_in, sp), (sf_in, sf)))
    ]
    for load in loads:
        load.start()

    barrier = pltpu.get_barrier_semaphore()
    for k in sorted(range(1, NDEV), key=lambda k: -hops(k)):
        pl.semaphore_signal(barrier, inc=1, device_id=peer(k), device_id_type=MESH)

    def remote(src, dst, send, recv, device):
        return pltpu.make_async_remote_copy(
            src_ref=src, dst_ref=dst, send_sem=send, recv_sem=recv, device_id=device, device_id_type=MESH
        )

    def group_rows(g):
        return pl.ds(16, 240) if g == 0 else pl.ds(g * 256, 256)

    def group_blocks(g):
        return pl.ds(1, 15) if g == 0 else pl.ds(g * 16, 16)

    orders = [sorted((k for k in range(g * GROUP, (g + 1) * GROUP) if k), key=lambda k: -hops(k)) for g in range(NGROUP)]

    me = s * 8 + t
    my_place = place_of(me)
    me_bits = [(my_place // (1 << b)) % 2 for b in range(7)]
    s_blk_row, s_rank_row, s_blk_col, s_rank_col, s_cl_col = slots_of(scl[...], me_bits)
    t_blk_row, t_rank_row, t_blk_col, t_rank_col, t_cl_col = slots_of(tcl[...], me_bits)
    s_slot_row = s_blk_row * CAP + s_rank_row
    t_slot_row = t_blk_row * CAP + t_rank_row
    s_slot_col = s_blk_col * CAP + s_rank_col

    lane = iota((ROWS, NDEV), 1)
    blk = iota((NDEV, ROWS), 0)
    s_val = jnp.where(lane == s_rank_col, (s_cl_col % CL_DEV + 1).astype(F32), 0.0).astype(BF)
    t_val = jnp.where(lane == t_rank_col + CAP, (t_cl_col % CL_DEV + 1).astype(F32), 0.0).astype(BF)
    s_hot = jnp.where(blk == s_blk_row, 1.0, 0.0).astype(BF)
    t_hot = jnp.where(blk == t_blk_row, 1.0, 0.0).astype(BF)
    labels = (dot(s_hot, s_val) + dot(t_hot, t_val)).astype(I32)
    ls[...] = labels.reshape(NDEV, 1, NDEV)
    lr[0] = ls[0]

    loads[0].wait()
    loads[1].wait()
    part = dot(tf[...], tp[...], ((0,), (0,)))
    pf[0] = part
    pp[0] = part.astype(BF)
    loads[2].wait()
    loads[3].wait()
    part = dot(sf[...], sp[...], ((0,), (0,)))
    pf[1] = part
    pp[1] = part.astype(BF)

    row = iota((ROWS, ROWS), 0)
    col = iota((ROWS, ROWS), 1)
    to_wire = jnp.where(col == (row // 4 % 4) * 64 + (row // 16) * 4 + row % 4, 1.0, 0.0).astype(BF)
    from_wire = jnp.where(row == (col // 4 % 4) * 64 + (col // 16) * 4 + col % 4, 1.0, 0.0).astype(BF)

    def hot_rows(g, slot_row):
        return jnp.where(iota((64, ROWS), 0) + g * 64 == slot_row, 1.0, 0.0).astype(BF)

    def quarters(x):
        return jnp.concatenate([x[:, q * QUART : (q + 1) * QUART] for q in range(4)], axis=0)

    def rows_of(x):
        return jnp.concatenate([x[q * 64 : (q + 1) * 64] for q in range(4)], axis=1)

    def pack_tgt(g):
        t_sel = hot_rows(g, t_slot_row)
        s_sel = hot_rows(g, s_slot_row)
        rows = dot(t_sel, tp[...]).astype(BF)
        f_t = dot(t_sel, tf[...]).astype(BF)
        f_s = dot(s_sel, sf[...]).astype(BF)
        facs = jnp.concatenate([f_s[:, :128], f_s[:, 128:], f_t[:, :128], f_t[:, 128:]], axis=0)
        at = slice(g * 256, (g + 1) * 256)
        ts[at, 0:QUART] = dot(to_wire, quarters(rows)).astype(BF)
        ts[at, QUART : QUART + 128] = dot(to_wire, facs).astype(BF)
        if g == 0:
            tr[0:16, :] = ts[0:16, :]

    def pack_src(g):
        rows = dot(hot_rows(g, s_slot_row), sp[...]).astype(BF)
        ss[g * 256 : (g + 1) * 256, :] = dot(to_wire, quarters(rows)).astype(BF)
        if g == 0:
            sr[0:16, :] = ss[0:16, :]

    def send_tgt(g):
        for k in orders[g]:
            at = pl.ds(k * 16, 16)
            remote(ts.at[at], tr.at[at], tg_s.at[g], tg_r.at[g], peer(k)).start()
            remote(ls.at[k], lr.at[k], lab_s.at[g], lab_r.at[g], peer(k)).start()

    def send_src(g):
        for k in orders[g]:
            at = pl.ds(k * 16, 16)
            remote(ss.at[at], sr.at[at], sc_s.at[g], sc_r.at[g], peer(k)).start()

    for g in GROUPS[:PACK_EARLY]:
        pack_tgt(g)

    pl.semaphore_wait(barrier, NDEV - 1)

    pair = remote(pp.at[1 - core], rx, pair_s, pair_r, partner)
    pair.start()

    for g in GROUPS[:SENT_FIRST]:
        send_tgt(g)
    for g in GROUPS[PACK_EARLY:PACK_PAIR]:
        pack_tgt(g)

    pair.wait_recv()
    cs[...] = (pf[core] + rx[...].astype(F32)).astype(BF)

    for kc in chips:
        ds, dz = kc // 4, kc % 4
        remote(
            cs.at[pl.ds(pl.multiple_of(sx[ds] * 16, 16), 16), pl.ds(pl.multiple_of(zx[dz] * 256, 256), 256)],
            rr.at[kc], rs_s, rs_r, (sx[ds], tx[dz * 2]),
        ).start()

    for g in GROUPS[SENT_FIRST:PACK_PAIR]:
        send_tgt(g)
    for i in range(PACK_PAIR, NGROUP):
        pack_tgt(GROUPS[i])
        send_tgt(GROUPS[i])
    for g in GROUPS:
        pack_src(g)

    rest = rr.at[pl.ds(1, 63)]
    remote(rest, rest, rs_s, rs_r, partner).wait_recv()
    my_rows = pl.ds(pl.multiple_of(s * 16, 16), 16)
    my_cols = pl.ds(pl.multiple_of(z * 256, 256), 256)
    total = cs[my_rows, my_cols].astype(F32)
    for kc in range(1, 64):
        total = total + rr[kc].astype(F32)
    mm[core, my_rows, my_cols] = total.astype(BF)

    mine = mm.at[core, my_rows, my_cols]
    for kc in chips:
        ds, dz = kc // 4, kc % 4
        remote(mine, mine, ag_s, ag_r, (sx[ds], tx[dz * 2])).start()
    for g in GROUPS[:SRC_NOW]:
        send_src(g)

    def owner_tgt(g):
        at = slice(g * 256, (g + 1) * 256)
        to = slice(g * 64, (g + 1) * 64)
        remote(ts.at[group_rows(g)], tr.at[group_rows(g)], tg_s.at[g], tg_r.at[g], partner).wait_recv()
        remote(ls.at[group_blocks(g)], lr.at[group_blocks(g)], lab_s.at[g], lab_r.at[g], partner).wait_recv()
        tall[to, :] = rows_of(dot(from_wire, tr[at, 0:QUART]).astype(BF))
        facs = dot(from_wire, tr[at, QUART : QUART + 128]).astype(BF)
        sfall[to, :] = jnp.concatenate([facs[0:64], facs[64:128]], axis=1)
        tfall[to, :] = jnp.concatenate([facs[128:192], facs[192:256]], axis=1)

    for i, g in enumerate(GROUPS):
        owner_tgt(g)
        if i == MID_AT:
            for h in GROUPS[SRC_NOW:SRC_MID]:
                send_src(h)

    remote(rest, rest, ag_s, ag_r, partner).wait_recv()
    pair_back = remote(mm.at[core], mm.at[core], pb_s, pb_r, partner)
    pair_back.start()

    for g in GROUPS[SRC_MID:]:
        send_src(g)

    def squares_of(points):
        total = jnp.zeros((points.shape[0], 128), F32)
        for j in range(D // 128):
            piece = points[:, j * 128 : (j + 1) * 128].astype(F32)
            total = total + piece * piece
        return total

    sums = dot(jnp.ones((8, 128), F32), squares_of(tall[...]), ((1,), (1,)), precision=lax.Precision.HIGHEST)
    inv_tgt = lax.rsqrt(sums + EPS)[0:1, :]

    got = lr[...].reshape(NDEV, NDEV).astype(F32).astype(BF)
    spread = jnp.where(iota((SLOTS, NDEV), 0) // CAP == iota((SLOTS, NDEV), 1), 1.0, 0.0).astype(BF)
    per_slot = dot(spread, got)
    slot_lane = iota((SLOTS, NDEV), 1) - iota((SLOTS, NDEV), 0) % CAP
    src_lab = jnp.sum(jnp.where(slot_lane == 0, per_slot, 0.0), axis=1, keepdims=True)
    tgt_lab = jnp.where(slot_lane == CAP, per_slot, 0.0).astype(BF)
    tgt_lab = dot(jnp.ones((8, NDEV), BF), tgt_lab, ((1,), (1,)))[0:1, :]

    remote(mm.at[1 - core], mm.at[1 - core], pb_s, pb_r, partner).wait_recv()
    marginal = marg[...]
    ball[...] = mirror(tall[...], mm[1], tfall[...], marginal)

    span = 64 * STEP

    def owner_src(groups):
        lo = min(groups)
        at0 = lo * 64
        pieces = [rows_of(dot(from_wire, sr[g * 256 : (g + 1) * 256, :]).astype(BF)) for g in sorted(groups)]
        points = jnp.concatenate(pieces, axis=0)
        update = mirror(points, mm[0], sfall[at0 : at0 + span, :], marginal)
        inv_src = lax.rsqrt(jnp.sum(squares_of(points), axis=1, keepdims=True) + EPS)
        cosine = dot(points, tall[...], ((1,), (1,))) * inv_src * inv_tgt
        weight = dot(update, ball[...], ((1,), (1,))) / R
        same = src_lab[at0 : at0 + span] == tgt_lab
        kern = jnp.where(same, weight * jnp.exp((cosine - 1.0) / TEMPER), 0.0)
        denominator = jnp.sum(kern, axis=1, keepdims=True)
        denominator = jnp.where(denominator > 0, denominator, 1.0)
        transport = (kern / denominator).astype(BF)
        image = dot(transport, tall[...]).astype(BF)
        for j, g in enumerate(sorted(groups)):
            isend[g * 256 : (g + 1) * 256, :] = dot(to_wire, quarters(image[j * 64 : (j + 1) * 64])).astype(BF)

    for first in range(0, NGROUP, STEP):
        groups = GROUPS[first : first + STEP]
        for g in groups:
            remote(ss.at[group_rows(g)], sr.at[group_rows(g)], sc_s.at[g], sc_r.at[g], partner).wait_recv()
        owner_src(groups)
        if 0 in groups:
            irecv[0:16, :] = isend[0:16, :]
        for g in groups:
            for k in orders[g]:
                at = pl.ds(k * 16, 16)
                remote(isend.at[at], irecv.at[at], rt_s.at[g], rt_r.at[g], peer(k)).start()

    su[...] = mirror(sp[...], mm[0], sf[...], marginal)
    tu[...] = mirror(tp[...], mm[1], tf[...], marginal)

    mapped = jnp.zeros((ROWS, D), F32)
    for first in range(0, NGROUP, LAST):
        groups = sorted(GROUPS[first : first + LAST])
        blocks = []
        for g in groups:
            remote(isend.at[group_rows(g)], irecv.at[group_rows(g)], rt_s.at[g], rt_r.at[g], partner).wait_recv()
            blocks.append(rows_of(dot(from_wire, irecv[g * 256 : (g + 1) * 256, :]).astype(BF)))
        images = jnp.concatenate(blocks, axis=0)
        pick = jnp.where(iota((ROWS, 64 * LAST), 1) + groups[0] * 64 == s_slot_col, 1.0, 0.0).astype(BF)
        mapped = mapped + dot(pick, images)
    mp[...] = mapped.astype(BF)

    pair.wait_send()
    remote(rest, rest, rs_s, rs_r, partner).wait_send()
    remote(rest, rest, ag_s, ag_r, partner).wait_send()
    pair_back.wait_send()
    for g in range(NGROUP):
        remote(ts.at[group_rows(g)], tr.at[group_rows(g)], tg_s.at[g], tg_r.at[g], partner).wait_send()
        remote(ls.at[group_blocks(g)], lr.at[group_blocks(g)], lab_s.at[g], lab_r.at[g], partner).wait_send()
        remote(ss.at[group_rows(g)], sr.at[group_rows(g)], sc_s.at[g], sc_r.at[g], partner).wait_send()
        remote(isend.at[group_rows(g)], irecv.at[group_rows(g)], rt_s.at[g], rt_r.at[g], partner).wait_send()


def put_out(su, tu, mp, su_out, tu_out, mp_out, sems):
    copies = [
        pltpu.make_async_copy(src, dst, sems.at[j])
        for j, (src, dst) in enumerate(((mp, mp_out), (su, su_out), (tu, tu_out)))
    ]
    for copy in copies:
        copy.start()
    for copy in copies:
        copy.wait()


def per_device(src_points, tgt_points, src_factor, tgt_factor, inner_marginal, src_cluster, tgt_cluster):
    dma = pltpu.SemaphoreType.DMA
    vmem = pl.BlockSpec(memory_space=pltpu.VMEM)
    hbm = pl.BlockSpec(memory_space=pl.ANY)
    su, tu, mp = pl.pallas_call(
        kernel,
        out_shape=(
            pltpu.VMEM((ROWS, R), BF),
            pltpu.VMEM((ROWS, R), BF),
            pltpu.VMEM((ROWS, D), BF),
        ),
        in_specs=[hbm] * 4 + [vmem] * 3,
        out_specs=(vmem,) * 3,
        scratch_shapes=[
            pltpu.VMEM((ROWS, D), BF),
            pltpu.VMEM((ROWS, D), BF),
            pltpu.VMEM((ROWS, R), BF),
            pltpu.VMEM((ROWS, R), BF),
            pltpu.VMEM((2, R, D), F32),
            pltpu.VMEM((2, R, D), BF),
            pltpu.VMEM((R, D), BF),
            pltpu.VMEM((R, D), BF),
            pltpu.VMEM((64, 16, 256), BF),
            pltpu.VMEM((2, R, D), BF),
            pltpu.VMEM((NDEV * 16, 384), BF),
            pltpu.VMEM((NDEV * 16, 384), BF),
            pltpu.VMEM((NDEV * 16, 256), BF),
            pltpu.VMEM((NDEV * 16, 256), BF),
            pltpu.VMEM((NDEV, 1, NDEV), I32),
            pltpu.VMEM((NDEV, 1, NDEV), I32),
            pltpu.VMEM((SLOTS, D), BF),
            pltpu.VMEM((SLOTS, R), BF),
            pltpu.VMEM((SLOTS, R), BF),
            pltpu.VMEM((SLOTS, R), BF),
            pltpu.VMEM((NDEV * 16, 256), BF),
            pltpu.VMEM((NDEV * 16, 256), BF),
        ]
        + [dma((4,))]
        + [dma] * 8
        + [dma((NGROUP,))] * 8,
        compiler_params=pltpu.CompilerParams(collective_id=0, has_side_effects=True, vmem_limit_bytes=VLIM),
        name="transport",
    )(
        src_points,
        tgt_points,
        src_factor,
        tgt_factor,
        inner_marginal.reshape(1, R),
        src_cluster.reshape(1, ROWS),
        tgt_cluster.reshape(1, ROWS),
    )
    shape = jax.ShapeDtypeStruct
    return pl.pallas_call(
        put_out,
        out_shape=(shape((ROWS, R), BF), shape((ROWS, R), BF), shape((ROWS, D), BF)),
        in_specs=[vmem] * 3,
        out_specs=(hbm,) * 3,
        scratch_shapes=[dma((3,))],
        name="put_out",
    )(*(pltpu.with_memory_space_constraint(x, pltpu.VMEM) for x in (su, tu, mp)))


def solution(mesh):
    both = P(("src", "tgt"), None)
    flat = P(("src", "tgt"))
    return jax.shard_map(
        per_device,
        mesh=mesh,
        in_specs=(both, both, both, both, P(), flat, flat),
        out_specs=(both, both, both),
        check_vma=False,
    )
```
